32 devices in a mesh: dp: 16 (over z, y, x), tensor: 2 (over core).
Axes of the slice: x: 2, y: 2, z: 4, core: 2. Of those that a mesh axis runs over, the one named last changes fastest.
Arguments:
- pool: bfloat16 [4096, 2048], P('dp', 'tensor'), may hold values from -6 to 6
- select: int32 [2048], P('dp'), may hold values from 0 to 4095, as said below
- reward_w: bfloat16 [2048], P('tensor'), may hold values from -0.125 to 0.125
- routes: int32 [2048, 6], P('dp'), may hold values from 0 to 15, all different within a row; in each aligned block of 128 rows (0 to 127, 128 to 255, ...) at most 60 rows name the same one
- gates: float32 [2048, 6], P('dp'), may hold values from 0.05 to 0.5
- target: bfloat16 [2048, 2048], P('dp', 'tensor'), may hold values from -6 to 6
- w_gate: bfloat16 [16, 1408, 2048], P('dp', 'tensor'), may hold values from -0.125 to 0.125
- w_up: bfloat16 [16, 1408, 2048], P('dp', 'tensor'), may hold values from -0.125 to 0.125
- w_down: bfloat16 [16, 1408, 2048], P('dp', 'tensor'), may hold values from -0.15625 to 0.15625
Outputs:
- mixed: bfloat16 [2048, 2048], P('dp', 'tensor')
- grad_gate: bfloat16 [16, 1408, 2048], P('dp', 'tensor')
- grad_up: bfloat16 [16, 1408, 2048], P('dp', 'tensor')
- grad_down: bfloat16 [16, 1408, 2048], P('dp', 'tensor')
The draws below stay inside these ranges and needn't reach their ends.
Inputs may be any that keep to these rules, and one draw needn't show every extreme that they name: The 128 entries of aligned block i of select are distinct rows of pool's block i, rows i * 256 to (i + 1) * 256 - 1. `routes`: each row names 6 different experts. In the 128 rows of one device no expert is named more than 60 times, a bound that some block reaches.
All inputs are finite; a program needn't handle non-finite values.
Results may differ from the reference program's by a relative error of at most 0.015.
Values may be sent and summed in bfloat16 or wider, within the bound.
A program may use at most 128 MiB of HBM per device.

```python
import math
import jax
import jax.numpy as jnp
import numpy as np
from jax import lax

D = 2048
FF = 1408
TOPK = 6
SEL_DEV = 128
POOL_DEV = 256
EXPERTS = 16
CAP = 60
SEL = 2048
POOL = 4096
N_TENSOR = 2


def draw_select(key, part):
    block_count = SEL // SEL_DEV

    def one_block(block_key):
        first_key, second_key, third_key = jax.random.split(block_key, 3)
        inner = jax.random.permutation(first_key, POOL_DEV - 2)[:SEL_DEV].astype(jnp.int32) + 1
        lowest = jax.random.randint(second_key, (), 0, SEL_DEV)
        highest = (lowest + 1 + jax.random.randint(third_key, (), 0, SEL_DEV - 1)) % SEL_DEV
        inner = inner.at[lowest].set(0)
        inner = inner.at[highest].set(POOL_DEV - 1)
        return inner.astype(jnp.int32)
    block_keys = jax.random.split(jax.random.fold_in(key, 11), block_count)
    local_rows = jax.vmap(one_block)(block_keys)
    offsets = jnp.arange(block_count, dtype=jnp.int32)[:, None] * POOL_DEV
    return (local_rows + offsets).reshape(SEL).astype(jnp.int32)


def levels(rng, shape, cuts, low, high):
    loudness, own = 1.0, jax.random.fold_in(rng, 6)
    for position, blocks in cuts:
        heights = jnp.exp(jax.random.uniform(jax.random.fold_in(own, position), (blocks,), jnp.float32, low / len(cuts), high / len(cuts)))
        loudness = loudness * jnp.repeat(heights, shape[position] // blocks).reshape([-1 if axis == position else 1 for axis in range(len(shape))])
    return loudness


def deal_out(own_key, own, number, rows, count, top, bound, skew):
    sequence = jax.random.permutation(own_key, count)
    packed, ordinary = shares(count, rows * top, bound, skew, True), shares(count, rows * top, bound, skew, False)
    places = jnp.arange(count)

    def named(sizes, turn):
        used = int((sizes > 0).sum())
        fixed = max(1, used // 4)
        moved = fixed + (places - fixed + turn * (used - fixed)) % max(1, count - fixed)
        return jnp.zeros((count,), jnp.int32).at[sequence[jnp.where(places < fixed, places, moved)]].set(jnp.asarray(sizes, jnp.int32))

    sizes = jnp.where(number % 4 == 0, named(packed, number // 4), named(ordinary, number - number // 4 - 1))
    mixed = jax.random.permutation(jax.random.fold_in(own, 3), count)
    donor, receiver = mixed[0:count // 2 * 2:2], mixed[1:count // 2 * 2:2]
    slack = jnp.minimum(sizes[donor] - 1, bound - sizes[receiver]) // 2
    slack = jnp.where((donor == sequence[0]) | (receiver == sequence[0]) | (sizes[receiver] == 0), 0, jnp.maximum(slack, 0))
    moved = jax.random.randint(jax.random.fold_in(own, 4), (count // 2,), 0, 1 << 20) % (slack + 1)
    sizes = sizes.at[donor].add(-moved).at[receiver].add(moved)
    members = jnp.searchsorted(jnp.cumsum(sizes), jnp.arange(rows * top), side="right").astype(jnp.int32)
    grid = members.reshape(top, rows).T
    grid = grid[jax.random.permutation(jax.random.fold_in(own, 1), rows)]
    turn = jax.random.randint(jax.random.fold_in(own, 2), (rows, 1), 0, top)
    return jnp.take_along_axis(grid, (jnp.arange(top)[None, :] + turn) % top, axis=1)


def shares(count, total, limit, skew, full):
    weights = [(1 << 20) // math.isqrt(rank ** skew) + 1 for rank in range(1, count + 1)]
    largest = limit if full else min(limit, max(-(-total // count), total * weights[0] // sum(weights)))
    least = 1 if total - largest >= count - 1 else 0
    holding, spare = [largest] + [least] * (count - 1), total - largest - least * (count - 1)
    while spare > 0:
        free = [i for i in range(1, count) if holding[i] < largest] or [i for i in range(1, count) if holding[i] < limit]
        mass, left = sum([weights[i] for i in free]), spare
        for i in free:
            more = min(limit - holding[i], max(1, left * weights[i] // mass), spare)
            holding[i] = holding[i] + more
            spare = spare - more
    return np.array(holding)


def scatter_about(key, dims, scale, reach, shards=(), kind=jnp.bfloat16):
    drawn = scale * jax.random.normal(key, dims, jnp.float32)
    if shards:
        drawn = drawn * levels(key, dims, shards, -0.22, 0.18)
    return jnp.clip(drawn, -reach, reach).astype(kind)


def setup_inputs(seed: int = 0) -> dict:
    key_list = jax.random.split(jax.random.key(seed), 10)
    pool = scatter_about(key_list[0], (POOL, D), 1.0, 6.0, ((0, 16), (1, 2)))
    select = draw_select(jax.random.fold_in(key_list[9], 71), 0)
    reward_w = scatter_about(key_list[2], (D,), D ** -0.5, 0.125, ((0, 2),))
    routes_keys = jax.random.split(jax.random.fold_in(key_list[3], 1), SEL // SEL_DEV)
    routes_turns = jax.random.permutation(jax.random.fold_in(key_list[3], 3), SEL // SEL_DEV)
    routes = jax.vmap(lambda own, number: deal_out(jax.random.fold_in(key_list[3], 2), own, number, SEL_DEV, EXPERTS, TOPK, CAP, 2))(routes_keys, routes_turns).reshape((SEL, TOPK))
    gates = jnp.clip(jnp.exp(math.log(0.5) - 2.3025851 * jax.random.uniform(key_list[4], (SEL, TOPK), jnp.float32) ** levels(key_list[4], (SEL, TOPK), ((0, 16),), -0.2, 0.2)), 0.05, 0.5)
    target = scatter_about(key_list[5], (SEL, D), 1.0, 6.0, ((0, 16), (1, 2)))
    w_gate = scatter_about(key_list[6], (EXPERTS, FF, D), D ** -0.5, 0.125, ((0, 16), (1, 2)))
    w_up = scatter_about(key_list[7], (EXPERTS, FF, D), D ** -0.5, 0.125, ((0, 16), (1, 2)))
    w_down = scatter_about(key_list[8], (EXPERTS, FF, D), FF ** -0.5, 0.15625, ((0, 16), (1, 2)))
    return {"pool": pool, "select": select, "reward_w": reward_w, "routes": routes, "gates": gates, "target": target, "w_gate": w_gate, "w_up": w_up, "w_down": w_down}


def reference(pool, select, reward_w, routes, gates, target, w_gate, w_up, w_down):
    chosen = pool[select]
    reward = jnp.dot(chosen, reward_w, preferred_element_type=jnp.float32)
    keep_scale = jax.nn.sigmoid(reward)
    route_cot = ((keep_scale[:, None] * gates)[:, :, None] * target.astype(jnp.float32)[:, None, :]).astype(jnp.bfloat16)
    cot_flat = route_cot.reshape(SEL * TOPK, D)
    block_count = SEL // SEL_DEV
    flat_routes = routes.reshape(block_count, SEL_DEV * TOPK)
    onehot = (flat_routes[:, :, None] == jnp.arange(EXPERTS, dtype=jnp.int32)[None, None, :]).astype(jnp.int32)
    slot_rank = jnp.sum((jnp.cumsum(onehot, axis=1) - onehot) * onehot, axis=2)
    column = (jnp.arange(block_count, dtype=jnp.int32)[:, None] * CAP + slot_rank).astype(jnp.int32)
    route_ids = jnp.arange(SEL * TOPK, dtype=jnp.int32).reshape(block_count, SEL_DEV * TOPK)
    slot_table = jnp.full((EXPERTS, block_count * CAP), SEL * TOPK, jnp.int32).at[flat_routes, column].set(route_ids)

    def expert(operands):
        slot_ids, gate_mat, up_mat, down_mat = operands
        live_rows = slot_ids < SEL * TOPK
        safe_ids = jnp.where(live_rows, slot_ids, 0)
        expert_rows = chosen[safe_ids // TOPK] * live_rows[:, None].astype(chosen.dtype)
        expert_cot = cot_flat[safe_ids] * live_rows[:, None].astype(cot_flat.dtype)
        gate_act = jnp.dot(expert_rows, gate_mat.T, preferred_element_type=jnp.float32)
        up_act = jnp.dot(expert_rows, up_mat.T, preferred_element_type=jnp.float32)
        sigmoid_gate = jax.nn.sigmoid(gate_act)
        hidden = (jax.nn.silu(gate_act) * up_act).astype(jnp.bfloat16)
        grouped = hidden.reshape(-1, N_TENSOR, FF // N_TENSOR).astype(jnp.float32)
        down_groups = down_mat.reshape(N_TENSOR, FF // N_TENSOR, D).astype(jnp.float32)
        group_sums = jnp.einsum("rgf,gfd->grd", grouped, down_groups)
        rounded = lax.optimization_barrier(group_sums.astype(jnp.bfloat16))
        expert_out = jnp.sum(rounded.astype(jnp.float32), axis=0).astype(jnp.bfloat16)
        hidden_grad = jnp.dot(expert_cot, down_mat.T, preferred_element_type=jnp.float32)
        gate_grad = (hidden_grad * up_act * sigmoid_gate * (1.0 + gate_act * (1.0 - sigmoid_gate))).astype(jnp.bfloat16)
        up_grad = (hidden_grad * jax.nn.silu(gate_act)).astype(jnp.bfloat16)
        grad_down = jnp.dot(hidden.T, expert_cot, preferred_element_type=jnp.float32).astype(jnp.bfloat16)
        grad_gate = jnp.dot(gate_grad.T, expert_rows, preferred_element_type=jnp.float32).astype(jnp.bfloat16)
        grad_up = jnp.dot(up_grad.T, expert_rows, preferred_element_type=jnp.float32).astype(jnp.bfloat16)
        return expert_out, grad_gate, grad_up, grad_down

    outputs, grad_gate, grad_up, grad_down = lax.map(expert, (slot_table, w_gate, w_up, w_down))
    route_out = outputs[flat_routes, column].reshape(SEL, TOPK, D).astype(jnp.float32)
    mixed = jnp.sum(route_out * gates[:, :, None], axis=1).astype(jnp.bfloat16)
    return mixed, grad_gate, grad_up, grad_down
```

```python
import functools
import jax
import jax.numpy as jnp
from jax import lax
from jax.experimental import pallas as pl
from jax.experimental.pallas import tpu as pltpu
from jax.sharding import PartitionSpec as P

MESH = pl.DeviceIdType.MESH
PLANE = 4
LINE = 4
PARTS = 2
F32 = jnp.float32
BF16 = jnp.bfloat16


def slot_factor(route_hit, weights):
    return jnp.sum(jnp.where(route_hit, weights.reshape(-1)[:, None], 0.0), axis=0)


def generic(pool, select, reward_w, routes, gates, target, w_gate, w_up, w_down):
    pool_rows = pool.shape[0]
    local_rows = select - lax.axis_index("dp") * pool_rows
    chosen = jnp.take(pool, local_rows, axis=0)
    sel_rows, top_count = routes.shape
    owners = lax.axis_size("dp")
    exp_dev = w_gate.shape[0]
    experts = owners * exp_dev
    capacity = 5 * sel_rows * top_count // (4 * experts)
    slot_count = experts * capacity
    flat_routes = routes.reshape(-1)
    onehot = (flat_routes[:, None] == jnp.arange(experts, dtype=jnp.int32)[None, :]).astype(
        jnp.int32
    )
    before = jnp.cumsum(onehot, axis=0) - onehot
    slot_rank = jnp.sum(before * onehot, axis=1)
    slot_place = flat_routes * capacity + slot_rank
    route_hit = slot_place[:, None] == jnp.arange(slot_count, dtype=jnp.int32)[None, :]
    route_pick = route_hit.astype(jnp.bfloat16).reshape(sel_rows, top_count, slot_count)
    token_pick = jnp.sum(route_pick, axis=1)
    reward = lax.psum(jnp.dot(chosen, reward_w, preferred_element_type=jnp.float32), "tensor")
    keep_scale = jax.nn.sigmoid(reward)
    slot_scale = slot_factor(route_hit, keep_scale[:, None] * gates)
    token_send = jnp.einsum(
        "sp,sd->pd", token_pick, chosen, preferred_element_type=jnp.float32
    ).astype(jnp.bfloat16)
    picked_target = jnp.einsum("sp,sd->pd", token_pick, target, preferred_element_type=jnp.float32)
    cot_send = (picked_target * slot_scale[:, None]).astype(jnp.bfloat16)
    token_part, cot_part = (
        lax.all_to_all(token_send, "dp", split_axis=0, concat_axis=0, tiled=True),
        lax.all_to_all(cot_send, "dp", split_axis=0, concat_axis=0, tiled=True),
    )
    received_tokens, received_cots = (
        lax.all_gather(token_part, "tensor", axis=1, tiled=True),
        lax.all_gather(cot_part, "tensor", axis=1, tiled=True),
    )
    width = received_tokens.shape[1]
    token_rows = received_tokens.reshape(owners, exp_dev, capacity, width)
    cot_rows = received_cots.reshape(owners, exp_dev, capacity, width)
    gate_act = jnp.einsum("secd,efd->secf", token_rows, w_gate, preferred_element_type=jnp.float32)
    up_act = jnp.einsum("secd,efd->secf", token_rows, w_up, preferred_element_type=jnp.float32)
    sigmoid_gate = jax.nn.sigmoid(gate_act)
    hidden = (gate_act * sigmoid_gate * up_act).astype(jnp.bfloat16)
    partial_value = jnp.einsum("secf,efd->secd", hidden, w_down, preferred_element_type=jnp.float32)
    summed = lax.psum_scatter(
        partial_value.astype(jnp.bfloat16), "tensor", scatter_dimension=3, tiled=True
    )
    returned = lax.all_to_all(summed, "dp", split_axis=0, concat_axis=0, tiled=True).reshape(
        slot_count, -1
    )
    route_rows = jnp.einsum("skp,pd->skd", route_pick, returned, preferred_element_type=jnp.float32)
    mixed = jnp.sum(route_rows * gates[:, :, None], axis=1).astype(jnp.bfloat16)
    hidden_grad = jnp.einsum("secd,efd->secf", cot_rows, w_down, preferred_element_type=jnp.float32)
    gate_grad = (
        hidden_grad * up_act * sigmoid_gate * (1.0 + gate_act * (1.0 - sigmoid_gate))
    ).astype(jnp.bfloat16)
    up_grad = (hidden_grad * gate_act * sigmoid_gate).astype(jnp.bfloat16)
    grad_down = jnp.einsum(
        "secf,secd->efd", hidden, cot_rows, preferred_element_type=jnp.float32
    ).astype(jnp.bfloat16)
    grad_gate = jnp.einsum(
        "secf,secd->efd", gate_grad, token_rows, preferred_element_type=jnp.float32
    ).astype(jnp.bfloat16)
    grad_up = jnp.einsum(
        "secf,secd->efd", up_grad, token_rows, preferred_element_type=jnp.float32
    ).astype(jnp.bfloat16)
    return (mixed, grad_gate, grad_up, grad_down)


def place():
    d = lax.axis_index("dp")
    c = lax.axis_index("tensor")
    z, q = d // PLANE, d % PLANE
    y, x = q // 2, q % 2
    mates = [((y + ry) % 2) * 2 + (x + rx) % 2 for ry, rx in ((0, 1), (1, 0), (1, 1))]
    return d, c, z, q, mates


def greet(d, c, z, q, mates):
    barrier = pltpu.get_barrier_semaphore()
    for m in mates:
        pl.semaphore_signal(barrier, inc=1, device_id=(z * PLANE + m, c), device_id_type=MESH)
    pl.semaphore_signal(barrier, inc=1, device_id=(d, 1 - c), device_id_type=MESH)

    @pl.when(z > 0)
    def _():
        pl.semaphore_signal(barrier, inc=1, device_id=(d - PLANE, c), device_id_type=MESH)

    @pl.when(z < LINE - 1)
    def _():
        pl.semaphore_signal(barrier, inc=1, device_id=(d + PLANE, c), device_id_type=MESH)


def greeted(z):
    below, above = (z + LINE - 1) // LINE, (2 * LINE - 2 - z) // LINE
    pl.semaphore_wait(pltpu.get_barrier_semaphore(), 4 + below + above)


def remote(src, dst, send, recv, dev):
    return pltpu.make_async_remote_copy(
        src_ref=src, dst_ref=dst, send_sem=send, recv_sem=recv, device_id=dev, device_id_type=MESH
    )


def sigmoid(v):
    return 1.0 / (1.0 + jnp.exp(-v))


def chunks(capacity):
    ends = [(j + 1) * capacity // 16 * 16 for j in range(LINE - 1)]
    ends.append(-(-LINE * capacity // 16) * 16)
    offs = [0] + ends[:-1]
    return offs, [b - a for a, b in zip(offs, ends)]


def layer_kernel(
    capacity, pad, pool_hbm, sel_ref, rw_ref, rt_ref, gt_ref, target_hbm, wg_hbm, wu_hbm, wd_hbm,
    mixed_ref, gg_ref, gu_ref, gd_ref,
    pool_ref, rt_vmem, gt_vmem, tok, cot, gate_act, up_act, hid, ggrad, ugrad, val,
    data, side_ref, scale, part, part_in, stage,
    partner_in, back, plane_in, acc, out_stage, line_in,
    lsem, zsend, zrecv, ssend, srecv, csend, crecv, xsend, xrecv, tsend, trecv, psend, precv,
    vsend, vrecv, bsend, brecv, usend, urecv,
):
    d, c, z, q, mates = place()
    experts = LINE * PLANE
    sel_rows, half = mixed_ref.shape
    top = gt_ref.shape[0]
    wg, wu, wd = gg_ref.at[0], gu_ref.at[0], gd_ref.at[0]
    units, width = wg.shape
    span = PLANE * pad
    offs, sizes = chunks(capacity)
    rows = (tok, cot)
    mine = pl.ds(pl.multiple_of(c * half, half), half)
    other = pl.ds(pl.multiple_of((1 - c) * half, half), half)
    partner = (d, 1 - c)
    seq = (z, z + 1 - 2 * (z % 2), 2 - z // 2, 3 - 3 * (z // 2))
    piece = half // PARTS
    nt = (((1,), (1,)), ((), ()))
    tn = (((0,), (0,)), ((), ()))

    greet(d, c, z, q, mates)
    loads = [
        pltpu.make_async_copy(src, dst, lsem.at[i])
        for i, (src, dst) in enumerate((
            (pool_hbm, pool_ref), (target_hbm, data.at[1, z]), (wg_hbm.at[0], wg),
            (wu_hbm.at[0], wu), (wd_hbm.at[0], wd), (rt_ref, rt_vmem), (gt_ref, gt_vmem),
        ))
    ]
    for i in (5, 6, 0, 1, 2, 3, 4):
        loads[i].start()

    for j in range(LINE):
        if sizes[j] < pad:
            for a in (0, 1):
                rows[a][j, :, sizes[j] : pad, :] = jnp.zeros(
                    (PLANE, pad - sizes[j], width), BF16
                )
    loads[5].wait()
    loads[6].wait()
    expert_id = lax.broadcasted_iota(jnp.int32, (experts, sel_rows), 0)
    member = jnp.zeros((experts, sel_rows), F32)
    gate = jnp.zeros((experts, sel_rows), F32)
    for k in range(top):
        eq = rt_vmem[k : k + 1, :] == expert_id
        member = member + jnp.where(eq, 1.0, 0.0)
        gate = gate + jnp.where(eq, gt_vmem[k : k + 1, :], 0.0)
    tri = jnp.where(
        lax.broadcasted_iota(jnp.int32, (sel_rows, sel_rows), 0)
        < lax.broadcasted_iota(jnp.int32, (sel_rows, sel_rows), 1),
        1.0,
        0.0,
    ).astype(BF16)
    before = jnp.dot(member.astype(BF16), tri, preferred_element_type=F32)
    side_ref[z, 0:experts, :] = jnp.where(member > 0.5, before, -1024.0)
    side_ref[z, experts : 2 * experts, :] = gate

    pool_rows = pool_ref.shape[0]
    hit = (
        lax.broadcasted_iota(jnp.int32, (pool_rows, sel_rows), 0) == sel_ref[...] - d * pool_rows
    ).astype(F32).astype(BF16)
    loads[0].wait()
    chosen = lax.dot_general(
        hit, pool_ref[...], tn, preferred_element_type=F32
    ).astype(BF16)
    data[0, z] = chosen
    rw = rw_ref[...].astype(F32)
    rw_rows = jnp.concatenate(
        [jnp.broadcast_to(rw[i : i + 1, :], (16, rw.shape[1])) for i in range(rw.shape[0])],
        axis=1,
    ).astype(BF16)
    part[...] = lax.dot_general(rw_rows, chosen, nt, preferred_element_type=F32)

    def zcopy(a, s, way, kind):
        blk = z - way * s
        dev = (d + way * PLANE, c)
        w = (way + 1) // 2
        if kind == 1:
            spot = data.at[a, blk]
            return remote(spot, spot, zsend.at[a, w, s], zrecv.at[a, blk], dev)
        if a == 0:
            spot = side_ref.at[blk]
            return remote(spot, spot, ssend.at[w, s], srecv.at[blk], dev)
        spot = scale.at[blk]
        return remote(spot, spot, csend.at[w, s], crecv.at[blk], dev)

    def sends(s, way):
        blk, to = z - way * s, z + way
        return (blk >= 0) & (blk < LINE) & (to >= 0) & (to < LINE)

    def zstart(a, s, which=(0, 1)):
        for way in (1, -1):
            @pl.when(sends(s, way))
            def _():
                for i in which:
                    zcopy(a, s, way, i).start()

    def arrives(s, way):
        blk = z - way * (s + 1)
        return (blk >= 0) & (blk < LINE)

    def zwait(a, s):
        for way in (1, -1):
            @pl.when(arrives(s, way))
            def _():
                blk = z - way * (s + 1)
                remote(
                    data.at[a, blk], data.at[a, blk], zsend.at[a, 0, 0], zrecv.at[a, blk], partner
                ).wait_recv()
                if a == 0:
                    remote(
                        side_ref.at[blk], side_ref.at[blk], ssend.at[0, 0], srecv.at[blk], partner
                    ).wait_recv()
                else:
                    remote(
                        scale.at[blk], scale.at[blk], csend.at[0, 0], crecv.at[blk], partner
                    ).wait_recv()

    def tcopy(a, j, m):
        spot = rows[a].at[j, m, 0 : sizes[j], mine]
        return remote(spot, spot, tsend.at[a, j, m], trecv.at[a, j, m], partner)

    def tarrive(a, j):
        for m in range(PLANE):
            spot = rows[a].at[j, m, 0 : sizes[j], other]
            remote(spot, spot, tsend.at[a, j, m], trecv.at[a, j, m], partner).wait_recv()

    def xcopy(a, j, r):
        return remote(
            stage.at[a, j, r, 0 : sizes[j], :],
            rows[a].at[j, q, 0 : sizes[j], mine],
            xsend.at[a, j, r],
            xrecv.at[a, j, q],
            (z * PLANE + mates[r], c),
        )

    slot_id = lax.broadcasted_iota(jnp.int32, (pad, sel_rows), 0).astype(F32)

    def pick(a, j):
        size = sizes[j]
        sources = [(seq[i], float(offs[j] - capacity * i)) for i in ((j, j - 1) if j else (j,))]
        sides = (2, 0, 1, 3)
        hits, factors = [], []
        for r in sides:
            e = z * PLANE + (mates[r] if r < 3 else q)
            ms = [slot_id[:size] + base == side_ref[b, pl.ds(e, 1), :] for b, base in sources]
            hits.append(jnp.concatenate([jnp.where(m, 1.0, 0.0) for m in ms], axis=1))
            if a == 1:
                total = sum(
                    jnp.where(m, scale[b, pl.ds(e, 1), :], 0.0) for m, (b, _) in zip(ms, sources)
                )
                factors.append(jnp.sum(total, axis=1, keepdims=True))
        hits = jnp.concatenate(hits, axis=0).astype(BF16)
        if a == 1:
            factors = jnp.concatenate(factors, axis=0)
        cut = 256 if half % 256 == 0 else half
        for n in range(half // cut):
            cols = pl.ds(n * cut, cut)
            source = jnp.concatenate([data[a, b, :, cols] for b, _ in sources], axis=0)
            picked = jnp.dot(hits, source, preferred_element_type=F32)
            if a == 1:
                picked = picked * factors
            picked = picked.astype(BF16)
            for i, r in enumerate(sides):
                got = picked[i * size : (i + 1) * size]
                if r < 3:
                    stage[a, j, r, 0:size, cols] = got
                else:
                    spot = pl.ds(pl.multiple_of(c * half + n * cut, cut), cut)
                    rows[a][j, q, 0:size, spot] = got
        for r in (2, 0, 1):
            xcopy(a, j, r).start()
        tcopy(a, j, q).start()

    def forward(a, j):
        for r in (0, 1, 2):
            m = mates[r]
            remote(
                stage.at[a, j, r, 0 : sizes[j], :], rows[a].at[j, m, 0 : sizes[j], mine],
                xsend.at[a, j, r], xrecv.at[a, j, m], partner,
            ).wait_recv()
            tcopy(a, j, m).start()

    def vcopy(j):
        return remote(
            val.at[j, :, 0 : sizes[j], other], partner_in.at[j, :, 0 : sizes[j], :],
            vsend.at[j], vrecv.at[j], partner,
        )

    tile = 512 if half % 512 == 0 else half

    def group(j):
        lanes = pl.ds(j * span, span)
        tarrive(0, j)
        x = tok[j].reshape(span, width)
        g = lax.dot_general(wg[...], x, nt, preferred_element_type=F32)
        u = lax.dot_general(wu[...], x, nt, preferred_element_type=F32)
        gate_act[j] = g
        up_act[j] = u
        h = (g * sigmoid(g) * u).astype(BF16)
        hid[:, lanes] = h
        for side in (1 - c, c):
            for n in range(half // tile):
                cols = pl.ds(pl.multiple_of(side * half + n * tile, tile), tile)
                v = lax.dot_general(h, wd[:, cols], tn, preferred_element_type=F32)
                val[j, :, :, cols] = v.astype(BF16).reshape(PLANE, pad, tile)
            if side is not c:
                vcopy(j).start()

    def grad_group(j):
        lanes = pl.ds(j * span, span)
        tarrive(1, j)
        x = cot[j].reshape(span, width)
        hg = lax.dot_general(wd[...], x, nt, preferred_element_type=F32)
        g = gate_act[j]
        s = sigmoid(g)
        ggrad[:, lanes] = (hg * up_act[j] * s * (1.0 + g * (1.0 - s))).astype(BF16)
        ugrad[:, lanes] = (hg * g * s).astype(BF16)

    grads = ((ggrad, tok, wg), (ugrad, tok, wu), (hid, cot, wd))
    strip = 256 if width % 256 == 0 else width
    strips = width // strip

    def grad_strip(n, carry):
        cols = pl.ds(pl.multiple_of(n * strip, strip), strip)
        for left, right, out in grads:
            r = right[:, :, :, cols].reshape(experts * pad, strip)
            out[:, cols] = jnp.dot(left[...], r, preferred_element_type=F32).astype(BF16)
        return carry

    def bcopy(j, r, h):
        cols = pl.ds(h * piece, piece)
        return remote(
            back.at[j, r, 0 : sizes[j], cols], plane_in.at[j, q, 0 : sizes[j], cols],
            bsend.at[j, r, h], brecv.at[j, q, h],
            (z * PLANE + mates[r], c),
        )

    def give(j):
        size = sizes[j]
        vcopy(j).wait_recv()
        for h in range(PARTS):
            cols = pl.ds(h * piece, piece)
            spot = pl.ds(pl.multiple_of(c * half + h * piece, piece), piece)
            for r in (2, 0, 1, 3):
                m = mates[r] if r < 3 else q
                total = (
                    val[j, m, 0:size, spot].astype(F32) + partner_in[j, m, 0:size, cols].astype(F32)
                ).astype(BF16)
                if r < 3:
                    back[j, r, 0:size, cols] = total
                    bcopy(j, r, h).start()
                else:
                    plane_in[j, q, 0:size, cols] = total

    def combine(j):
        blk = seq[j]
        weights, takes = [], []
        for m in range(PLANE):
            e = z * PLANE + m
            rank = side_ref[blk, pl.ds(e, 1), :]
            strength = side_ref[blk, pl.ds(experts + e, 1), :]
            spots = [(j, sizes[j])] + ([(j + 1, 16)] if j + 1 < LINE else [])
            for i, size in spots:
                base = float(offs[i] - capacity * j)
                w = jnp.where(slot_id[:size] + base == rank, strength, 0.0)
                high = w.astype(BF16)
                weights += [high, (w - high.astype(F32)).astype(BF16)]
                takes += [(i, m, size)] * 2
        weights = jnp.concatenate(weights, axis=0)
        for h in range(PARTS):
            cols = pl.ds(h * piece, piece)
            for r in range(3):
                remote(
                    back.at[j, r, 0 : sizes[j], cols], plane_in.at[j, mates[r], 0 : sizes[j], cols],
                    bsend.at[j, r, h], brecv.at[j, mates[r], h], partner,
                ).wait_recv()
            values = jnp.concatenate(
                [plane_in[i, m, 0:size, cols] for i, m, size in takes], axis=0
            )
            acc[blk, :, cols] = lax.dot_general(weights, values, tn, preferred_element_type=F32)

    def ucopy(w, s, h):
        cols = pl.ds(h * piece, piece)
        to = d + (2 * w - 1) * PLANE
        return remote(
            out_stage.at[w, s, :, cols], line_in.at[w, s, :, cols], usend.at[w, s, h],
            urecv.at[w, s, h], (to, c),
        )

    def height(w):
        return z if w == 1 else LINE - 1 - z

    def lifts(w, s):
        return (height(w) <= s) & (height(w) < LINE - 1)

    def lands(w, s):
        return (height(w) > 0) & (height(w) - 1 <= s)

    def lift(s):
        for w in (1, 0):
            blk = z + (2 * w - 1) * (LINE - 1 - s)
            for h in range(PARTS):
                cols = pl.ds(h * piece, piece)
                if s > 0:
                    @pl.when(lands(w, s - 1))
                    def _():
                        ucopy(w, s - 1, h).wait_recv()

                    @pl.when(lifts(w, s) & (height(w) > 0))
                    def _():
                        out_stage[w, s, :, cols] = (
                            acc[blk, :, cols] + line_in[w, s - 1, :, cols].astype(F32)
                        ).astype(BF16)
                        ucopy(w, s, h).start()

                @pl.when(lifts(w, s) & (height(w) == 0))
                def _():
                    out_stage[w, s, :, cols] = acc[blk, :, cols].astype(BF16)
                    ucopy(w, s, h).start()

    greeted(z)
    reward_copy = remote(part, part_in, psend, precv, partner)
    reward_copy.start()
    zstart(0, 0)
    pick(0, 0)
    loads[1].wait()
    zstart(1, 0, (1,))
    reward_copy.wait()
    scale[z] = sigmoid(part[0:1, :] + part_in[0:1, :]) * side_ref[z, experts : 2 * experts, :]
    zstart(1, 0, (0,))
    pick(1, 0)
    forward(0, 0)
    zwait(0, 0)
    zstart(0, 1)
    pick(0, 1)
    for cp in loads[2:5]:
        cp.wait()
    group(0)
    forward(1, 0)
    zwait(1, 0)
    pick(1, 1)
    grad_group(0)
    forward(0, 1)
    zwait(0, 1)
    zstart(0, 2)
    zstart(1, 1)
    pick(0, 2)
    group(1)
    forward(1, 1)
    zwait(0, 2)
    pick(0, 3)
    grad_group(1)
    forward(0, 2)
    zwait(1, 1)
    zstart(1, 2)
    pick(1, 2)
    group(2)
    forward(0, 3)
    zwait(1, 2)
    pick(1, 3)
    group(3)
    for j in (3, 2, 1, 0):
        give(j)
    forward(1, 2)
    grad_group(2)
    forward(1, 3)
    grad_group(3)

    last = LINE - 2
    done = 0
    for s in range(LINE - 1):
        upto = strips * (s + 1) // (LINE - 1)
        combine(LINE - 1 - s)
        lift(s)
        lax.fori_loop(done, upto, grad_strip, 0)
        done = upto
    combine(0)
    for h in range(PARTS):
        cols = pl.ds(h * piece, piece)
        for w in (1, 0):
            @pl.when(lands(w, last))
            def _():
                ucopy(w, last, h).wait_recv()
                acc[z, :, cols] = acc[z, :, cols] + line_in[w, last, :, cols].astype(F32)
        mixed_ref[:, cols] = acc[z, :, cols].astype(BF16)

    for j in range(LINE):
        vcopy(j).wait_send()
        for a in (0, 1):
            for m in range(PLANE):
                tcopy(a, j, m).wait_send()
        for r in range(3):
            for h in range(PARTS):
                bcopy(j, r, h).wait_send()
            for a in (0, 1):
                xcopy(a, j, r).wait_send()
    for s in range(LINE - 1):
        for w in (1, 0):
            @pl.when(lifts(w, s))
            def _():
                for h in range(PARTS):
                    ucopy(w, s, h).wait_send()

        for a in (0, 1):
            for way in (1, -1):
                @pl.when(sends(s, way))
                def _():
                    for kind in (0, 1):
                        zcopy(a, s, way, kind).wait_send()


def flush_kernel(*refs):
    count = len(refs) // 2
    sem = refs[-1]
    copies = []
    for i in range(count):
        src, dst = refs[i], refs[count + i]
        for j in range(PARTS):
            cut = pl.ds(j * (src.shape[-2] // PARTS), src.shape[-2] // PARTS)
            at = (cut,) if len(src.shape) == 2 else (0, cut)
            copies.append(pltpu.make_async_copy(src.at[at], dst.at[at], sem.at[i, j]))
    for cp in copies:
        cp.start()
    for cp in copies:
        cp.wait()


def flush(*outs):
    return pl.pallas_call(
        flush_kernel,
        name="flush",
        out_shape=tuple(jax.ShapeDtypeStruct(o.shape, o.dtype) for o in outs),
        in_specs=vmem(len(outs)),
        out_specs=tuple(hbm(len(outs))),
        scratch_shapes=[DMA((len(outs), PARTS))],
        compiler_params=pltpu.CompilerParams(vmem_limit_bytes=1 << 20),
    )(*[pltpu.with_memory_space_constraint(o, pltpu.VMEM) for o in outs])


def vmem(count):
    return [pl.BlockSpec(memory_space=pltpu.VMEM)] * count


def hbm(count):
    return [pl.BlockSpec(memory_space=pl.ANY)] * count


DMA = pltpu.SemaphoreType.DMA


def planar(pool, select, reward_w, routes, gates, target, w_gate, w_up, w_down):
    experts = LINE * PLANE
    sel_rows, top = routes.shape
    capacity = 5 * sel_rows * top // (4 * experts)
    pad = max(chunks(capacity)[1])
    half = target.shape[1]
    units, width = w_gate.shape[1:]
    span = PLANE * pad
    grad_shape = pltpu.VMEM(w_gate.shape, BF16)
    rw = reward_w.reshape(half // 128, 128)
    slots = pltpu.VMEM((LINE, PLANE, pad, width), BF16)
    act = pltpu.VMEM((LINE, units, span), F32)
    flat = pltpu.VMEM((units, experts * pad), BF16)
    outs = pl.pallas_call(
        functools.partial(layer_kernel, capacity, pad),
        name="layer",
        out_shape=(pltpu.VMEM((sel_rows, half), BF16), grad_shape, grad_shape, grad_shape),
        in_specs=hbm(1) + vmem(2) + hbm(6),
        out_specs=tuple(vmem(4)),
        scratch_shapes=[
            pltpu.VMEM(pool.shape, BF16), pltpu.VMEM((top, sel_rows), jnp.int32),
            pltpu.VMEM((top, sel_rows), F32), slots, slots, act, act, flat, flat, flat, slots,
            pltpu.VMEM((2, LINE, sel_rows, half), BF16),
            pltpu.VMEM((LINE, 2 * experts, sel_rows), F32),
            pltpu.VMEM((LINE, experts, sel_rows), F32),
            pltpu.VMEM((16, sel_rows), F32),
            pltpu.VMEM((16, sel_rows), F32),
            pltpu.VMEM((2, LINE, 3, pad, half), BF16),
            pltpu.VMEM((LINE, PLANE, pad, half), BF16),
            pltpu.VMEM((LINE, 3, pad, half), BF16),
            pltpu.VMEM((LINE, PLANE, pad, half), BF16),
            pltpu.VMEM((LINE, sel_rows, half), F32),
            pltpu.VMEM((2, LINE - 1, sel_rows, half), BF16),
            pltpu.VMEM((2, LINE - 1, sel_rows, half), BF16),
            DMA((7,)),
            DMA((2, 2, LINE)), DMA((2, LINE)), DMA((2, LINE)), DMA((LINE,)),
            DMA((2, LINE)), DMA((LINE,)), DMA((2, LINE, 3)), DMA((2, LINE, PLANE)),
            DMA((2, LINE, PLANE)), DMA((2, LINE, PLANE)), DMA, DMA,
            DMA((LINE,)), DMA((LINE,)), DMA((LINE, 3, PARTS)), DMA((LINE, PLANE, PARTS)),
            DMA((2, LINE, PARTS)), DMA((2, LINE, PARTS)),
        ],
        compiler_params=pltpu.CompilerParams(
            collective_id=0, has_side_effects=True, vmem_limit_bytes=57 * 10**6
        ),
    )(pool, select.reshape(1, sel_rows), rw, routes.T, gates.T, target,
      w_gate, w_up, w_down)
    return flush(*outs)


def solution(mesh):
    in_specs = (
        P("dp", "tensor"), P("dp"), P("tensor"), P("dp", None), P("dp", None), P("dp", "tensor"),
        P("dp", "tensor", None), P("dp", "tensor", None), P("dp", "tensor", None),
    )
    out_specs = (
        P("dp", "tensor"), P("dp", "tensor", None), P("dp", "tensor", None),
        P("dp", "tensor", None),
    )
    dp, tensor = mesh.shape["dp"], mesh.shape["tensor"]
    fits = tensor == 2 and dp == LINE * PLANE
    local = planar if fits else generic
    return jax.shard_map(local, mesh=mesh, in_specs=in_specs, out_specs=out_specs, check_vma=False)
```

```python
import functools
import jax
import jax.numpy as jnp
from jax import lax
from jax.experimental import pallas as pl
from jax.experimental.pallas import tpu as pltpu
from jax.sharding import PartitionSpec as P

MESH = pl.DeviceIdType.MESH
PLANE = 4
LINE = 4
PARTS = 2
F32 = jnp.float32
BF16 = jnp.bfloat16


def slot_factor(route_hit, weights):
    return jnp.sum(jnp.where(route_hit, weights.reshape(-1)[:, None], 0.0), axis=0)


def generic(pool, select, reward_w, routes, gates, target, w_gate, w_up, w_down):
    pool_rows = pool.shape[0]
    local_rows = select - lax.axis_index("dp") * pool_rows
    chosen = jnp.take(pool, local_rows, axis=0)
    sel_rows, top_count = routes.shape
    owners = lax.axis_size("dp")
    exp_dev = w_gate.shape[0]
    experts = owners * exp_dev
    capacity = 5 * sel_rows * top_count // (4 * experts)
    slot_count = experts * capacity
    flat_routes = routes.reshape(-1)
    onehot = (flat_routes[:, None] == jnp.arange(experts, dtype=jnp.int32)[None, :]).astype(
        jnp.int32
    )
    before = jnp.cumsum(onehot, axis=0) - onehot
    slot_rank = jnp.sum(before * onehot, axis=1)
    slot_place = flat_routes * capacity + slot_rank
    route_hit = slot_place[:, None] == jnp.arange(slot_count, dtype=jnp.int32)[None, :]
    route_pick = route_hit.astype(jnp.bfloat16).reshape(sel_rows, top_count, slot_count)
    token_pick = jnp.sum(route_pick, axis=1)
    reward = lax.psum(jnp.dot(chosen, reward_w, preferred_element_type=jnp.float32), "tensor")
    keep_scale = jax.nn.sigmoid(reward)
    slot_scale = slot_factor(route_hit, keep_scale[:, None] * gates)
    token_send = jnp.einsum(
        "sp,sd->pd", token_pick, chosen, preferred_element_type=jnp.float32
    ).astype(jnp.bfloat16)
    picked_target = jnp.einsum("sp,sd->pd", token_pick, target, preferred_element_type=jnp.float32)
    cot_send = (picked_target * slot_scale[:, None]).astype(jnp.bfloat16)
    token_part, cot_part = (
        lax.all_to_all(token_send, "dp", split_axis=0, concat_axis=0, tiled=True),
        lax.all_to_all(cot_send, "dp", split_axis=0, concat_axis=0, tiled=True),
    )
    received_tokens, received_cots = (
        lax.all_gather(token_part, "tensor", axis=1, tiled=True),
        lax.all_gather(cot_part, "tensor", axis=1, tiled=True),
    )
    width = received_tokens.shape[1]
    token_rows = received_tokens.reshape(owners, exp_dev, capacity, width)
    cot_rows = received_cots.reshape(owners, exp_dev, capacity, width)
    gate_act = jnp.einsum("secd,efd->secf", token_rows, w_gate, preferred_element_type=jnp.float32)
    up_act = jnp.einsum("secd,efd->secf", token_rows, w_up, preferred_element_type=jnp.float32)
    sigmoid_gate = jax.nn.sigmoid(gate_act)
    hidden = (gate_act * sigmoid_gate * up_act).astype(jnp.bfloat16)
    partial_value = jnp.einsum("secf,efd->secd", hidden, w_down, preferred_element_type=jnp.float32)
    summed = lax.psum_scatter(
        partial_value.astype(jnp.bfloat16), "tensor", scatter_dimension=3, tiled=True
    )
    returned = lax.all_to_all(summed, "dp", split_axis=0, concat_axis=0, tiled=True).reshape(
        slot_count, -1
    )
    route_rows = jnp.einsum("skp,pd->skd", route_pick, returned, preferred_element_type=jnp.float32)
    mixed = jnp.sum(route_rows * gates[:, :, None], axis=1).astype(jnp.bfloat16)
    hidden_grad = jnp.einsum("secd,efd->secf", cot_rows, w_down, preferred_element_type=jnp.float32)
    gate_grad = (
        hidden_grad * up_act * sigmoid_gate * (1.0 + gate_act * (1.0 - sigmoid_gate))
    ).astype(jnp.bfloat16)
    up_grad = (hidden_grad * gate_act * sigmoid_gate).astype(jnp.bfloat16)
    grad_down = jnp.einsum(
        "secf,secd->efd", hidden, cot_rows, preferred_element_type=jnp.float32
    ).astype(jnp.bfloat16)
    grad_gate = jnp.einsum(
        "secf,secd->efd", gate_grad, token_rows, preferred_element_type=jnp.float32
    ).astype(jnp.bfloat16)
    grad_up = jnp.einsum(
        "secf,secd->efd", up_grad, token_rows, preferred_element_type=jnp.float32
    ).astype(jnp.bfloat16)
    return (mixed, grad_gate, grad_up, grad_down)


def place():
    d = lax.axis_index("dp")
    c = lax.axis_index("tensor")
    z, q = d // PLANE, d % PLANE
    y, x = q // 2, q % 2
    mates = [((y + ry) % 2) * 2 + (x + rx) % 2 for ry, rx in ((0, 1), (1, 0), (1, 1))]
    return d, c, z, q, mates


def greet(d, c, z, q, mates):
    barrier = pltpu.get_barrier_semaphore()
    for m in mates:
        pl.semaphore_signal(barrier, inc=1, device_id=(z * PLANE + m, c), device_id_type=MESH)
    pl.semaphore_signal(barrier, inc=1, device_id=(d, 1 - c), device_id_type=MESH)

    @pl.when(z > 0)
    def _():
        pl.semaphore_signal(barrier, inc=1, device_id=(d - PLANE, c), device_id_type=MESH)

    @pl.when(z < LINE - 1)
    def _():
        pl.semaphore_signal(barrier, inc=1, device_id=(d + PLANE, c), device_id_type=MESH)


def greeted(z):
    below, above = (z + LINE - 1) // LINE, (2 * LINE - 2 - z) // LINE
    pl.semaphore_wait(pltpu.get_barrier_semaphore(), 4 + below + above)


def remote(src, dst, send, recv, dev):
    return pltpu.make_async_remote_copy(
        src_ref=src, dst_ref=dst, send_sem=send, recv_sem=recv, device_id=dev, device_id_type=MESH
    )


def sigmoid(v):
    return 1.0 / (1.0 + jnp.exp(-v))


def chunks(capacity):
    ends = [(j + 1) * capacity // 16 * 16 for j in range(LINE - 1)]
    ends.append(-(-LINE * capacity // 16) * 16)
    offs = [0] + ends[:-1]
    return offs, [b - a for a, b in zip(offs, ends)]


def layer_kernel(
    capacity, pad, pool_hbm, sel_hbm, rw_hbm, rt_hbm, gt_hbm, target_hbm, wg_hbm, wu_hbm, wd_hbm,
    mixed_ref, gg_ref, gu_ref, gd_ref, tok, cot, hid, ggrad, ugrad,
    pool_ref, sel_ref, rw_ref, rt_ref, gt_ref, gate_act, up_act, val,
    data, side_ref, scale, part, part_in, stage,
    partner_in, back, plane_in, acc, out_stage, line_in,
    lsem, zsend, zrecv, ssend, srecv, csend, crecv, xsend, xrecv, tsend, trecv, psend, precv,
    vsend, vrecv, bsend, brecv, usend, urecv,
):
    d, c, z, q, mates = place()
    experts = LINE * PLANE
    sel_rows, half = mixed_ref.shape
    top = gt_hbm.shape[0]
    wg, wu, wd = gg_ref.at[0], gu_ref.at[0], gd_ref.at[0]
    units, width = wg.shape
    span = PLANE * pad
    offs, sizes = chunks(capacity)
    rows = (tok, cot)
    mine = pl.ds(pl.multiple_of(c * half, half), half)
    other = pl.ds(pl.multiple_of((1 - c) * half, half), half)
    partner = (d, 1 - c)
    seq = (z, z + 1 - 2 * (z % 2), 2 - z // 2, 3 - 3 * (z // 2))
    piece = half // PARTS
    nt = (((1,), (1,)), ((), ()))
    tn = (((0,), (0,)), ((), ()))

    greet(d, c, z, q, mates)
    loads = [
        pltpu.make_async_copy(src, dst, lsem.at[i])
        for i, (src, dst) in enumerate((
            (sel_hbm, sel_ref), (pool_hbm, pool_ref), (rt_hbm, rt_ref), (gt_hbm, gt_ref),
            (rw_hbm, rw_ref), (target_hbm, data.at[1, z]), (wg_hbm.at[0], wg), (wu_hbm.at[0], wu),
            (wd_hbm.at[0], wd),
        ))
    ]
    for cp in loads:
        cp.start()

    loads[0].wait()
    pool_rows = pool_ref.shape[0]
    hit = (
        lax.broadcasted_iota(jnp.int32, (pool_rows, sel_rows), 0) == sel_ref[...] - d * pool_rows
    ).astype(F32).astype(BF16)
    loads[1].wait()
    chosen = lax.dot_general(
        hit, pool_ref[...], tn, preferred_element_type=F32
    ).astype(BF16)
    data[0, z] = chosen

    def zcopy(a, s, way, kind):
        blk = z - way * s
        dev = (d + way * PLANE, c)
        w = (way + 1) // 2
        if kind == 1:
            spot = data.at[a, blk]
            return remote(spot, spot, zsend.at[w], zrecv.at[a, blk], dev)
        if a == 0:
            spot = side_ref.at[blk]
            return remote(spot, spot, ssend.at[w], srecv.at[blk], dev)
        spot = scale.at[blk]
        return remote(spot, spot, csend.at[w], crecv.at[blk], dev)

    def sends(s, way):
        blk, to = z - way * s, z + way
        return (blk >= 0) & (blk < LINE) & (to >= 0) & (to < LINE)

    def zstart(a, s, which=(0, 1)):
        for way in (1, -1):
            @pl.when(sends(s, way))
            def _():
                for i in which:
                    zcopy(a, s, way, i).start()

    def arrives(s, way):
        blk = z - way * (s + 1)
        return (blk >= 0) & (blk < LINE)

    def zwait(a, s):
        for way in (1, -1):
            @pl.when(arrives(s, way))
            def _():
                blk = z - way * (s + 1)
                remote(
                    data.at[a, blk], data.at[a, blk], zsend.at[0], zrecv.at[a, blk], partner
                ).wait_recv()
                if a == 0:
                    remote(
                        side_ref.at[blk], side_ref.at[blk], ssend.at[0], srecv.at[blk], partner
                    ).wait_recv()
                else:
                    remote(
                        scale.at[blk], scale.at[blk], csend.at[0], crecv.at[blk], partner
                    ).wait_recv()

    def tcopy(a, j, m):
        spot = rows[a].at[j, m, 0 : sizes[j], mine]
        return remote(spot, spot, tsend.at[a, min(j, 1)], trecv.at[a, j], partner)

    def tall(a, j, side):
        spot = rows[a].at[j, :, 0 : sizes[j], side]
        return remote(spot, spot, tsend.at[a, min(j, 1)], trecv.at[a, j], partner)

    def tarrive(a, j):
        tall(a, j, other).wait_recv()

    def xcopy(a, j, r):
        return remote(
            stage.at[a, j, r, 0 : sizes[j], :],
            rows[a].at[j, q, 0 : sizes[j], mine],
            xsend.at[min(j, 1)],
            xrecv.at[a, j],
            (z * PLANE + mates[r], c),
        )

    slot_id = lax.broadcasted_iota(jnp.int32, (pad, sel_rows), 0).astype(F32)

    def pick(a, j):
        size = sizes[j]
        sources = [(seq[i], float(offs[j] - capacity * i)) for i in ((j, j - 1) if j else (j,))]
        sides = (2, 0, 1, 3)
        hits, factors = [], []
        for r in sides:
            e = z * PLANE + (mates[r] if r < 3 else q)
            ms = [slot_id[:size] + base == side_ref[b, pl.ds(e, 1), :] for b, base in sources]
            hits.append(jnp.concatenate([jnp.where(m, 1.0, 0.0) for m in ms], axis=1))
            if a == 1:
                total = sum(
                    jnp.where(m, scale[b, pl.ds(e, 1), :], 0.0) for m, (b, _) in zip(ms, sources)
                )
                factors.append(jnp.sum(total, axis=1, keepdims=True))
        hits = jnp.concatenate(hits, axis=0).astype(BF16)
        if a == 1:
            factors = jnp.concatenate(factors, axis=0)
        cut = 256 if half % 256 == 0 else half
        for n in range(half // cut):
            cols = pl.ds(n * cut, cut)
            source = jnp.concatenate([data[a, b, :, cols] for b, _ in sources], axis=0)
            picked = jnp.dot(hits, source, preferred_element_type=F32)
            if a == 1:
                picked = picked * factors
            picked = picked.astype(BF16)
            for i, r in enumerate(sides):
                got = picked[i * size : (i + 1) * size]
                if r < 3:
                    stage[a, j, r, 0:size, cols] = got
                else:
                    spot = pl.ds(pl.multiple_of(c * half + n * cut, cut), cut)
                    rows[a][j, q, 0:size, spot] = got
        for r in (2, 0, 1):
            xcopy(a, j, r).start()
        tcopy(a, j, q).start()

    def forward(a, j):
        remote(
            stage.at[a, j, :, 0 : sizes[j], :], rows[a].at[j, 0:3, 0 : sizes[j], mine],
            xsend.at[min(j, 1)], xrecv.at[a, j], partner,
        ).wait_recv()
        for m in mates:
            tcopy(a, j, m).start()

    def vcopy(j):
        return remote(
            val.at[j, :, 0 : sizes[j], other], partner_in.at[j, :, 0 : sizes[j], :],
            vsend.at[min(j, 1)], vrecv.at[j], partner,
        )

    tile = 512 if half % 512 == 0 else half

    def group(j):
        lanes = pl.ds(j * span, span)
        tarrive(0, j)
        x = tok[j].reshape(span, width)
        g = lax.dot_general(wg[...], x, nt, preferred_element_type=F32)
        u = lax.dot_general(wu[...], x, nt, preferred_element_type=F32)
        gate_act[j] = g
        up_act[j] = u
        h = (g * sigmoid(g) * u).astype(BF16)
        hid[:, lanes] = h
        for side in (1 - c, c):
            for n in range(half // tile):
                cols = pl.ds(pl.multiple_of(side * half + n * tile, tile), tile)
                v = lax.dot_general(h, wd[:, cols], tn, preferred_element_type=F32)
                val[j, :, :, cols] = v.astype(BF16).reshape(PLANE, pad, tile)
            if side is not c:
                vcopy(j).start()

    def grad_group(j):
        lanes = pl.ds(j * span, span)
        tarrive(1, j)
        x = cot[j].reshape(span, width)
        hg = lax.dot_general(wd[...], x, nt, preferred_element_type=F32)
        g = gate_act[j]
        s = sigmoid(g)
        ggrad[:, lanes] = (hg * up_act[j] * s * (1.0 + g * (1.0 - s))).astype(BF16)
        ugrad[:, lanes] = (hg * g * s).astype(BF16)

    grads = ((ggrad, tok, wg), (ugrad, tok, wu), (hid, cot, wd))
    strip = 256 if width % 256 == 0 else width
    strips = width // strip - left_over(width // strip)

    def grad_strip(n, carry):
        cols = pl.ds(pl.multiple_of(n * strip, strip), strip)
        for left, right, out in grads:
            r = right[:, :, :, cols].reshape(experts * pad, strip)
            out[:, cols] = jnp.dot(left[...], r, preferred_element_type=F32).astype(BF16)
        return carry

    def bcopy(j, r, h):
        cols = pl.ds(h * piece, piece)
        return remote(
            back.at[j, r, 0 : sizes[j], cols], plane_in.at[j, q, 0 : sizes[j], cols],
            bsend.at[min(j, 1)], brecv.at[j, h],
            (z * PLANE + mates[r], c),
        )

    def give(j):
        size = sizes[j]
        vcopy(j).wait_recv()
        for h in range(PARTS):
            cols = pl.ds(h * piece, piece)
            spot = pl.ds(pl.multiple_of(c * half + h * piece, piece), piece)
            for r in (2, 0, 1, 3):
                m = mates[r] if r < 3 else q
                total = (
                    val[j, m, 0:size, spot].astype(F32) + partner_in[j, m, 0:size, cols].astype(F32)
                ).astype(BF16)
                if r < 3:
                    back[j, r, 0:size, cols] = total
                    bcopy(j, r, h).start()
                else:
                    plane_in[j, q, 0:size, cols] = total

    def mixing(j):
        blk = seq[j]
        weights, takes = [], []
        for m in range(PLANE):
            e = z * PLANE + m
            rank = side_ref[blk, pl.ds(e, 1), :]
            strength = side_ref[blk, pl.ds(experts + e, 1), :]
            spots = [(j, sizes[j])] + ([(j + 1, 16)] if j + 1 < LINE else [])
            for i, size in spots:
                base = float(offs[i] - capacity * j)
                w = jnp.where(slot_id[:size] + base == rank, strength, 0.0)
                high = w.astype(BF16)
                weights += [high, (w - high.astype(F32)).astype(BF16)]
                takes += [(i, m, size)] * 2
        return jnp.concatenate(weights, axis=0), takes

    def combine(j, h, mix):
        weights, takes = mix
        cols = pl.ds(h * piece, piece)
        remote(
            back.at[j, :, 0 : sizes[j], cols], plane_in.at[j, 0:3, 0 : sizes[j], cols],
            bsend.at[min(j, 1)], brecv.at[j, h], partner,
        ).wait_recv()
        values = jnp.concatenate([plane_in[i, m, 0:size, cols] for i, m, size in takes], axis=0)
        acc[seq[j], :, cols] = lax.dot_general(weights, values, tn, preferred_element_type=F32)

    def ucopy(w, s, h):
        cols = pl.ds(h * piece, piece)
        to = d + (2 * w - 1) * PLANE
        return remote(
            out_stage.at[w, s, :, cols], line_in.at[w, s, :, cols], usend.at[w],
            urecv.at[w, s, h], (to, c),
        )

    def height(w):
        return z if w == 1 else LINE - 1 - z

    def lifts(w, s):
        return (height(w) <= s) & (height(w) < LINE - 1)

    def lands(w, s):
        return (height(w) > 0) & (height(w) - 1 <= s)

    def lift(s, h):
        cols = pl.ds(h * piece, piece)
        for w in (1, 0):
            blk = z + (2 * w - 1) * (LINE - 1 - s)
            if s > 0:
                @pl.when(lands(w, s - 1))
                def _():
                    ucopy(w, s - 1, h).wait_recv()

                @pl.when(lifts(w, s) & (height(w) > 0))
                def _():
                    out_stage[w, s, :, cols] = (
                        acc[blk, :, cols] + line_in[w, s - 1, :, cols].astype(F32)
                    ).astype(BF16)
                    ucopy(w, s, h).start()

            @pl.when(lifts(w, s) & (height(w) == 0))
            def _():
                out_stage[w, s, :, cols] = acc[blk, :, cols].astype(BF16)
                ucopy(w, s, h).start()

    def sides():
        expert_id = lax.broadcasted_iota(jnp.int32, (experts, sel_rows), 0)
        member = jnp.zeros((experts, sel_rows), F32)
        gate = jnp.zeros((experts, sel_rows), F32)
        for k in range(top):
            eq = rt_ref[k : k + 1, :] == expert_id
            member = member + jnp.where(eq, 1.0, 0.0)
            gate = gate + jnp.where(eq, gt_ref[k : k + 1, :], 0.0)
        tri = jnp.where(
            lax.broadcasted_iota(jnp.int32, (sel_rows, sel_rows), 0)
            < lax.broadcasted_iota(jnp.int32, (sel_rows, sel_rows), 1),
            1.0,
            0.0,
        ).astype(BF16)
        before = jnp.dot(member.astype(BF16), tri, preferred_element_type=F32)
        side_ref[z, 0:experts, :] = jnp.where(member > 0.5, before, -1024.0)
        side_ref[z, experts : 2 * experts, :] = gate

    def rewards():
        rw = rw_ref[...].astype(F32)
        rw_rows = jnp.concatenate(
            [jnp.broadcast_to(rw[i : i + 1, :], (16, rw.shape[1])) for i in range(rw.shape[0])],
            axis=1,
        ).astype(BF16)
        part[...] = lax.dot_general(rw_rows, data[0, z], nt, preferred_element_type=F32)

    reward_copy = remote(part, part_in, psend, precv, partner)
    greeted(z)
    zstart(0, 0, (1,))
    loads[2].wait()
    loads[3].wait()
    sides()
    zstart(0, 0, (0,))
    loads[5].wait()
    zstart(1, 0, (1,))
    pick(0, 0)
    loads[4].wait()
    rewards()
    reward_copy.start()
    for j in range(LINE):
        if sizes[j] < pad:
            for a in (0, 1):
                rows[a][j, :, sizes[j] : pad, :] = jnp.zeros(
                    (PLANE, pad - sizes[j], width), BF16
                )
    reward_copy.wait()
    scale[z] = sigmoid(part[0:1, :] + part_in[0:1, :]) * side_ref[z, experts : 2 * experts, :]
    zstart(1, 0, (0,))
    pick(1, 0)
    forward(0, 0)
    zwait(0, 0)
    zstart(0, 1)
    pick(0, 1)
    for cp in loads[6:9]:
        cp.wait()
    group(0)
    forward(1, 0)
    zwait(1, 0)
    pick(1, 1)
    grad_group(0)
    forward(0, 1)
    zwait(0, 1)
    zstart(0, 2)
    zstart(1, 1)
    pick(0, 2)
    group(1)
    forward(1, 1)
    zwait(0, 2)
    pick(0, 3)
    grad_group(1)
    forward(0, 2)
    zwait(1, 1)
    zstart(1, 2)
    pick(1, 2)
    group(2)
    forward(0, 3)
    zwait(1, 2)
    pick(1, 3)
    group(3)
    for j in (3, 2, 1, 0):
        give(j)
    forward(1, 2)
    grad_group(2)
    forward(1, 3)
    grad_group(3)

    last = LINE - 2
    turns = (LINE - 1) * PARTS
    done, turn = 0, 0
    for s in range(LINE - 1):
        j = LINE - 1 - s
        mix = mixing(j)
        for h in range(PARTS):
            combine(j, h, mix)
            lift(s, h)
            upto = strips * turn // (turns - 2)
            upto = min(upto, strips)
            if upto > done:
                lax.fori_loop(done, upto, grad_strip, 0)
                done = upto
            turn = turn + 1
    lax.fori_loop(done, strips, grad_strip, 0)

    def sent(src, sem):
        remote(src, src, sem, vrecv.at[0], partner).wait_send()

    for w in (0, 1):
        for n in range(1, LINE):
            @pl.when(LINE - height(1 - w) == n)
            def _():
                sent(data.at[:, 0:n], zsend.at[w])
                sent(side_ref.at[0:n], ssend.at[w])
                sent(scale.at[0:n], csend.at[w])
    for i, cut in ((0, slice(0, 1)), (1, slice(1, LINE))):
        size = sizes[0] if i == 0 else pad
        sent(stage.at[:, cut, :, 0:size, :], xsend.at[i])
        sent(val.at[cut, :, 0:size, other], vsend.at[i])
        for a in (0, 1):
            sent(rows[a].at[cut, :, 0:size, mine], tsend.at[a, i])

    mix = mixing(0)
    for h in range(PARTS):
        combine(0, h, mix)
        cols = pl.ds(h * piece, piece)
        for w in (1, 0):
            @pl.when(lands(w, last))
            def _():
                ucopy(w, last, h).wait_recv()
                acc[z, :, cols] = acc[z, :, cols] + line_in[w, last, :, cols].astype(F32)
        mixed_ref[:, cols] = acc[z, :, cols].astype(BF16)

    for w in (0, 1):
        for n in range(1, LINE):
            @pl.when(LINE - 1 - height(w) == n)
            def _():
                sent(out_stage.at[w, 0:n], usend.at[w])
    sent(back.at[0:1, :, 0 : sizes[0], :], bsend.at[0])
    sent(back.at[1:LINE], bsend.at[1])


def left_over(strips):
    return strips // 4


def flush_kernel(
    mixed, gg, gu, gd, tok, cot, hid, ggrad, ugrad, mixed_out, gg_out, gu_out, gd_out, last, sem
):
    units, width = gg.shape[1:]
    late = last.shape[1] * last.shape[3]
    strip = last.shape[3]
    early = width - late
    rows = units // PARTS
    copies = [pltpu.make_async_copy(mixed, mixed_out, sem.at[0, 0])]
    grads = ((gg, gg_out, ggrad, tok), (gu, gu_out, ugrad, tok), (gd, gd_out, hid, cot))
    for i, (src, dst, _, _) in enumerate(grads):
        for p in range(PARTS):
            at = (0, pl.ds(p * rows, rows), pl.ds(0, early))
            copies.append(pltpu.make_async_copy(src.at[at], dst.at[at], sem.at[i + 1, p]))
    for cp in copies:
        cp.start()
    for n in range(last.shape[1]):
        cols = pl.ds(early + n * strip, strip)
        for i, (_, dst, left, right) in enumerate(grads):
            r = right[:, :, :, cols].reshape(left.shape[1], strip)
            last[i, n] = jnp.dot(left[...], r, preferred_element_type=F32).astype(BF16)
            cp = pltpu.make_async_copy(last.at[i, n], dst.at[0, :, cols], sem.at[i + 1, PARTS + n])
            cp.start()
            copies.append(cp)
    for cp in copies:
        cp.wait()


def flush(*outs):
    units, width = outs[1].shape[1:]
    strip = 256 if width % 256 == 0 else width
    late = left_over(width // strip)
    return pl.pallas_call(
        flush_kernel,
        name="flush",
        out_shape=tuple(jax.ShapeDtypeStruct(o.shape, o.dtype) for o in outs[:4]),
        in_specs=vmem(len(outs)),
        out_specs=tuple(hbm(4)),
        scratch_shapes=[pltpu.VMEM((3, late, units, strip), BF16), DMA((4, PARTS + late))],
        compiler_params=pltpu.CompilerParams(vmem_limit_bytes=12 << 20),
    )(*[pltpu.with_memory_space_constraint(o, pltpu.VMEM) for o in outs])


def vmem(count):
    return [pl.BlockSpec(memory_space=pltpu.VMEM)] * count


def hbm(count):
    return [pl.BlockSpec(memory_space=pl.ANY)] * count


DMA = pltpu.SemaphoreType.DMA


def planar(pool, select, reward_w, routes, gates, target, w_gate, w_up, w_down):
    experts = LINE * PLANE
    sel_rows, top = routes.shape
    capacity = 5 * sel_rows * top // (4 * experts)
    pad = max(chunks(capacity)[1])
    half = target.shape[1]
    units, width = w_gate.shape[1:]
    span = PLANE * pad
    grad_shape = pltpu.VMEM(w_gate.shape, BF16)
    rw = reward_w.reshape(half // 128, 128)
    slots = pltpu.VMEM((LINE, PLANE, pad, width), BF16)
    act = pltpu.VMEM((LINE, units, span), F32)
    flat = pltpu.VMEM((units, experts * pad), BF16)
    outs = pl.pallas_call(
        functools.partial(layer_kernel, capacity, pad),
        name="layer",
        out_shape=(
            pltpu.VMEM((sel_rows, half), BF16), grad_shape, grad_shape, grad_shape,
            slots, slots, flat, flat, flat,
        ),
        in_specs=hbm(9),
        out_specs=tuple(vmem(9)),
        scratch_shapes=[
            pltpu.VMEM(pool.shape, BF16), pltpu.VMEM((1, sel_rows), jnp.int32),
            pltpu.VMEM(rw.shape, BF16), pltpu.VMEM((top, sel_rows), jnp.int32),
            pltpu.VMEM((top, sel_rows), F32), act, act, slots,
            pltpu.VMEM((2, LINE, sel_rows, half), BF16),
            pltpu.VMEM((LINE, 2 * experts, sel_rows), F32),
            pltpu.VMEM((LINE, experts, sel_rows), F32),
            pltpu.VMEM((16, sel_rows), F32),
            pltpu.VMEM((16, sel_rows), F32),
            pltpu.VMEM((2, LINE, 3, pad, half), BF16),
            pltpu.VMEM((LINE, PLANE, pad, half), BF16),
            pltpu.VMEM((LINE, 3, pad, half), BF16),
            pltpu.VMEM((LINE, PLANE, pad, half), BF16),
            pltpu.VMEM((LINE, sel_rows, half), F32),
            pltpu.VMEM((2, LINE - 1, sel_rows, half), BF16),
            pltpu.VMEM((2, LINE - 1, sel_rows, half), BF16),
            DMA((9,)),
            DMA((2,)), DMA((2, LINE)), DMA((2,)), DMA((LINE,)),
            DMA((2,)), DMA((LINE,)), DMA((2,)), DMA((2, LINE)),
            DMA((2, 2)), DMA((2, LINE)), DMA, DMA,
            DMA((2,)), DMA((LINE,)), DMA((2,)), DMA((LINE, PARTS)),
            DMA((2,)), DMA((2, LINE - 1, PARTS)),
        ],
        compiler_params=pltpu.CompilerParams(
            collective_id=0, has_side_effects=True, vmem_limit_bytes=44 * 10**6
        ),
    )(pool, select.reshape(1, sel_rows), rw, routes.T, gates.T, target,
      w_gate, w_up, w_down)
    return flush(*outs)


def solution(mesh):
    in_specs = (
        P("dp", "tensor"), P("dp"), P("tensor"), P("dp", None), P("dp", None), P("dp", "tensor"),
        P("dp", "tensor", None), P("dp", "tensor", None), P("dp", "tensor", None),
    )
    out_specs = (
        P("dp", "tensor"), P("dp", "tensor", None), P("dp", "tensor", None),
        P("dp", "tensor", None),
    )
    dp, tensor = mesh.shape["dp"], mesh.shape["tensor"]
    fits = tensor == 2 and dp == LINE * PLANE
    local = planar if fits else generic
    return jax.shard_map(local, mesh=mesh, in_specs=in_specs, out_specs=out_specs, check_vma=False)
```

```python
import functools
import jax
import jax.numpy as jnp
from jax import lax
from jax.experimental import pallas as pl
from jax.experimental.pallas import tpu as pltpu
from jax.sharding import PartitionSpec as P

MESH = pl.DeviceIdType.MESH
PLANE = 4
LINE = 4
PARTS = 2
F32 = jnp.float32
BF16 = jnp.bfloat16


def slot_factor(route_hit, weights):
    return jnp.sum(jnp.where(route_hit, weights.reshape(-1)[:, None], 0.0), axis=0)


def generic(pool, select, reward_w, routes, gates, target, w_gate, w_up, w_down):
    pool_rows = pool.shape[0]
    local_rows = select - lax.axis_index("dp") * pool_rows
    chosen = jnp.take(pool, local_rows, axis=0)
    sel_rows, top_count = routes.shape
    owners = lax.axis_size("dp")
    exp_dev = w_gate.shape[0]
    experts = owners * exp_dev
    capacity = 5 * sel_rows * top_count // (4 * experts)
    slot_count = experts * capacity
    flat_routes = routes.reshape(-1)
    onehot = (flat_routes[:, None] == jnp.arange(experts, dtype=jnp.int32)[None, :]).astype(
        jnp.int32
    )
    before = jnp.cumsum(onehot, axis=0) - onehot
    slot_rank = jnp.sum(before * onehot, axis=1)
    slot_place = flat_routes * capacity + slot_rank
    route_hit = slot_place[:, None] == jnp.arange(slot_count, dtype=jnp.int32)[None, :]
    route_pick = route_hit.astype(jnp.bfloat16).reshape(sel_rows, top_count, slot_count)
    token_pick = jnp.sum(route_pick, axis=1)
    reward = lax.psum(jnp.dot(chosen, reward_w, preferred_element_type=jnp.float32), "tensor")
    keep_scale = jax.nn.sigmoid(reward)
    slot_scale = slot_factor(route_hit, keep_scale[:, None] * gates)
    token_send = jnp.einsum(
        "sp,sd->pd", token_pick, chosen, preferred_element_type=jnp.float32
    ).astype(jnp.bfloat16)
    picked_target = jnp.einsum("sp,sd->pd", token_pick, target, preferred_element_type=jnp.float32)
    cot_send = (picked_target * slot_scale[:, None]).astype(jnp.bfloat16)
    token_part, cot_part = (
        lax.all_to_all(token_send, "dp", split_axis=0, concat_axis=0, tiled=True),
        lax.all_to_all(cot_send, "dp", split_axis=0, concat_axis=0, tiled=True),
    )
    received_tokens, received_cots = (
        lax.all_gather(token_part, "tensor", axis=1, tiled=True),
        lax.all_gather(cot_part, "tensor", axis=1, tiled=True),
    )
    width = received_tokens.shape[1]
    token_rows = received_tokens.reshape(owners, exp_dev, capacity, width)
    cot_rows = received_cots.reshape(owners, exp_dev, capacity, width)
    gate_act = jnp.einsum("secd,efd->secf", token_rows, w_gate, preferred_element_type=jnp.float32)
    up_act = jnp.einsum("secd,efd->secf", token_rows, w_up, preferred_element_type=jnp.float32)
    sigmoid_gate = jax.nn.sigmoid(gate_act)
    hidden = (gate_act * sigmoid_gate * up_act).astype(jnp.bfloat16)
    partial_value = jnp.einsum("secf,efd->secd", hidden, w_down, preferred_element_type=jnp.float32)
    summed = lax.psum_scatter(
        partial_value.astype(jnp.bfloat16), "tensor", scatter_dimension=3, tiled=True
    )
    returned = lax.all_to_all(summed, "dp", split_axis=0, concat_axis=0, tiled=True).reshape(
        slot_count, -1
    )
    route_rows = jnp.einsum("skp,pd->skd", route_pick, returned, preferred_element_type=jnp.float32)
    mixed = jnp.sum(route_rows * gates[:, :, None], axis=1).astype(jnp.bfloat16)
    hidden_grad = jnp.einsum("secd,efd->secf", cot_rows, w_down, preferred_element_type=jnp.float32)
    gate_grad = (
        hidden_grad * up_act * sigmoid_gate * (1.0 + gate_act * (1.0 - sigmoid_gate))
    ).astype(jnp.bfloat16)
    up_grad = (hidden_grad * gate_act * sigmoid_gate).astype(jnp.bfloat16)
    grad_down = jnp.einsum(
        "secf,secd->efd", hidden, cot_rows, preferred_element_type=jnp.float32
    ).astype(jnp.bfloat16)
    grad_gate = jnp.einsum(
        "secf,secd->efd", gate_grad, token_rows, preferred_element_type=jnp.float32
    ).astype(jnp.bfloat16)
    grad_up = jnp.einsum(
        "secf,secd->efd", up_grad, token_rows, preferred_element_type=jnp.float32
    ).astype(jnp.bfloat16)
    return (mixed, grad_gate, grad_up, grad_down)


def place():
    d = lax.axis_index("dp")
    c = lax.axis_index("tensor")
    z, q = d // PLANE, d % PLANE
    y, x = q // 2, q % 2
    mates = [((y + ry) % 2) * 2 + (x + rx) % 2 for ry, rx in ((0, 1), (1, 0), (1, 1))]
    return d, c, z, q, mates


def greet(d, c, z, q, mates):
    barrier = pltpu.get_barrier_semaphore()
    for m in mates:
        pl.semaphore_signal(barrier, inc=1, device_id=(z * PLANE + m, c), device_id_type=MESH)
    pl.semaphore_signal(barrier, inc=1, device_id=(d, 1 - c), device_id_type=MESH)

    @pl.when(z > 0)
    def _():
        pl.semaphore_signal(barrier, inc=1, device_id=(d - PLANE, c), device_id_type=MESH)

    @pl.when(z < LINE - 1)
    def _():
        pl.semaphore_signal(barrier, inc=1, device_id=(d + PLANE, c), device_id_type=MESH)


def greeted(z):
    below, above = (z + LINE - 1) // LINE, (2 * LINE - 2 - z) // LINE
    pl.semaphore_wait(pltpu.get_barrier_semaphore(), 4 + below + above)


def remote(src, dst, send, recv, dev):
    return pltpu.make_async_remote_copy(
        src_ref=src, dst_ref=dst, send_sem=send, recv_sem=recv, device_id=dev, device_id_type=MESH
    )


def sigmoid(v):
    return 1.0 / (1.0 + jnp.exp(-v))


def chunks(capacity):
    ends = [(j + 1) * capacity // 16 * 16 for j in range(LINE - 1)]
    ends.append(-(-LINE * capacity // 16) * 16)
    offs = [0] + ends[:-1]
    return offs, [b - a for a, b in zip(offs, ends)]


def layer_kernel(
    capacity, pad, pool_hbm, sel_hbm, rw_hbm, rt_hbm, gt_hbm, target_hbm, wg_hbm, wu_hbm, wd_hbm,
    mixed_ref, gg_ref, gu_ref, gd_ref, tok, cot, hid, ggrad, ugrad,
    pool_ref, sel_ref, rw_ref, rt_ref, gt_ref, gate_act, up_act, val,
    data, side_ref, scale, part, part_in, stage,
    partner_in, back, plane_in, acc, out_stage, line_in,
    lsem, zsend, zrecv, ssend, srecv, csend, crecv, xsend, xrecv, tsend, trecv, psend, precv,
    vsend, vrecv, bsend, brecv, usend, urecv,
):
    d, c, z, q, mates = place()
    experts = LINE * PLANE
    sel_rows, half = mixed_ref.shape
    top = gt_hbm.shape[0]
    wg, wu, wd = gg_ref.at[0], gu_ref.at[0], gd_ref.at[0]
    units, width = wg.shape
    span = PLANE * pad
    offs, sizes = chunks(capacity)
    rows = (tok, cot)
    mine = pl.ds(pl.multiple_of(c * half, half), half)
    other = pl.ds(pl.multiple_of((1 - c) * half, half), half)
    partner = (d, 1 - c)
    seq = (z, z + 1 - 2 * (z % 2), 2 - z // 2, 3 - 3 * (z // 2))
    piece = half // PARTS
    nt = (((1,), (1,)), ((), ()))
    tn = (((0,), (0,)), ((), ()))

    greet(d, c, z, q, mates)
    loads = [
        pltpu.make_async_copy(src, dst, lsem.at[i])
        for i, (src, dst) in enumerate((
            (sel_hbm, sel_ref), (pool_hbm, pool_ref), (rt_hbm, rt_ref), (gt_hbm, gt_ref),
            (rw_hbm, rw_ref), (target_hbm, data.at[1, z]), (wg_hbm.at[0], wg), (wu_hbm.at[0], wu),
            (wd_hbm.at[0], wd),
        ))
    ]
    for cp in loads[:5]:
        cp.start()

    loads[0].wait()
    pool_rows = pool_ref.shape[0]
    hit = (
        lax.broadcasted_iota(jnp.int32, (pool_rows, sel_rows), 0) == sel_ref[...] - d * pool_rows
    ).astype(F32).astype(BF16)
    loads[1].wait()
    loads[5].start()
    chosen = lax.dot_general(
        hit, pool_ref[...], tn, preferred_element_type=F32
    ).astype(BF16)
    data[0, z] = chosen

    def zcopy(a, s, way, kind):
        blk = z - way * s
        dev = (d + way * PLANE, c)
        w = (way + 1) // 2
        if kind == 1:
            spot = data.at[a, blk]
            return remote(spot, spot, zsend.at[w], zrecv.at[a, blk], dev)
        if a == 0:
            spot = side_ref.at[blk]
            return remote(spot, spot, ssend.at[w], srecv.at[blk], dev)
        spot = scale.at[blk]
        return remote(spot, spot, csend.at[w], crecv.at[blk], dev)

    def inside(to):
        return (z > 0) & (z < LINE - 1) & (to > 0) & (to < LINE - 1)

    def among(links, to):
        return {"all": True, "inner": inside(to), "outer": jnp.logical_not(inside(to))}[links]

    def sends(s, way):
        blk, to = z - way * s, z + way
        return (blk >= 0) & (blk < LINE) & (to >= 0) & (to < LINE)

    def zstart(a, s, which=(0, 1), links="all"):
        for way in (1, -1):
            @pl.when(sends(s, way) & among(links, z + way))
            def _():
                for i in which:
                    zcopy(a, s, way, i).start()

    def arrives(s, way):
        blk = z - way * (s + 1)
        return (blk >= 0) & (blk < LINE)

    def zwait(a, s, links="all"):
        for way in (1, -1):
            @pl.when(arrives(s, way) & among(links, z - way))
            def _():
                blk = z - way * (s + 1)
                remote(
                    data.at[a, blk], data.at[a, blk], zsend.at[0], zrecv.at[a, blk], partner
                ).wait_recv()
                if a == 0:
                    remote(
                        side_ref.at[blk], side_ref.at[blk], ssend.at[0], srecv.at[blk], partner
                    ).wait_recv()
                else:
                    remote(
                        scale.at[blk], scale.at[blk], csend.at[0], crecv.at[blk], partner
                    ).wait_recv()

    def tcopy(a, j, m):
        spot = rows[a].at[j, m, 0 : sizes[j], mine]
        return remote(spot, spot, tsend.at[a, min(j, 1)], trecv.at[a, j], partner)

    def tall(a, j, side):
        spot = rows[a].at[j, :, 0 : sizes[j], side]
        return remote(spot, spot, tsend.at[a, min(j, 1)], trecv.at[a, j], partner)

    def tarrive(a, j):
        tall(a, j, other).wait_recv()

    def xcopy(a, j, r):
        return remote(
            stage.at[a, j, r, 0 : sizes[j], :],
            rows[a].at[j, q, 0 : sizes[j], mine],
            xsend.at[min(j, 1)],
            xrecv.at[a, j],
            (z * PLANE + mates[r], c),
        )

    slot_id = lax.broadcasted_iota(jnp.int32, (pad, sel_rows), 0).astype(F32)

    def pick(a, j):
        size = sizes[j]
        sources = [(seq[i], float(offs[j] - capacity * i)) for i in ((j, j - 1) if j else (j,))]
        sides = (2, 0, 1, 3)
        hits, factors = [], []
        for r in sides:
            e = z * PLANE + (mates[r] if r < 3 else q)
            ms = [slot_id[:size] + base == side_ref[b, pl.ds(e, 1), :] for b, base in sources]
            hits.append(jnp.concatenate([jnp.where(m, 1.0, 0.0) for m in ms], axis=1))
            if a == 1:
                total = sum(
                    jnp.where(m, scale[b, pl.ds(e, 1), :], 0.0) for m, (b, _) in zip(ms, sources)
                )
                factors.append(jnp.sum(total, axis=1, keepdims=True))
        hits = jnp.concatenate(hits, axis=0).astype(BF16)
        if a == 1:
            factors = jnp.concatenate(factors, axis=0)
        cut = 256 if half % 256 == 0 else half
        for n in range(half // cut):
            cols = pl.ds(n * cut, cut)
            source = jnp.concatenate([data[a, b, :, cols] for b, _ in sources], axis=0)
            picked = jnp.dot(hits, source, preferred_element_type=F32)
            if a == 1:
                picked = picked * factors
            picked = picked.astype(BF16)
            for i, r in enumerate(sides):
                got = picked[i * size : (i + 1) * size]
                if r < 3:
                    stage[a, j, r, 0:size, cols] = got
                else:
                    spot = pl.ds(pl.multiple_of(c * half + n * cut, cut), cut)
                    rows[a][j, q, 0:size, spot] = got
        for r in (2, 0, 1):
            xcopy(a, j, r).start()
        tcopy(a, j, q).start()

    def forward(a, j):
        remote(
            stage.at[a, j, :, 0 : sizes[j], :], rows[a].at[j, 0:3, 0 : sizes[j], mine],
            xsend.at[min(j, 1)], xrecv.at[a, j], partner,
        ).wait_recv()
        for m in mates:
            tcopy(a, j, m).start()

    def vcopy(j):
        return remote(
            val.at[j, :, 0 : sizes[j], other], partner_in.at[j, :, 0 : sizes[j], :],
            vsend.at[min(j, 1)], vrecv.at[j], partner,
        )

    tile = 512 if half % 512 == 0 else half

    def group(j):
        lanes = pl.ds(j * span, span)
        tarrive(0, j)
        x = tok[j].reshape(span, width)
        g = lax.dot_general(wg[...], x, nt, preferred_element_type=F32)
        u = lax.dot_general(wu[...], x, nt, preferred_element_type=F32)
        gate_act[j] = g
        up_act[j] = u
        h = (g * sigmoid(g) * u).astype(BF16)
        hid[:, lanes] = h
        for side in (1 - c, c):
            for n in range(half // tile):
                cols = pl.ds(pl.multiple_of(side * half + n * tile, tile), tile)
                v = lax.dot_general(h, wd[:, cols], tn, preferred_element_type=F32)
                val[j, :, :, cols] = v.astype(BF16).reshape(PLANE, pad, tile)
            if side is not c:
                vcopy(j).start()

    def grad_group(j):
        lanes = pl.ds(j * span, span)
        tarrive(1, j)
        x = cot[j].reshape(span, width)
        hg = lax.dot_general(wd[...], x, nt, preferred_element_type=F32)
        g = gate_act[j]
        s = sigmoid(g)
        ggrad[:, lanes] = (hg * up_act[j] * s * (1.0 + g * (1.0 - s))).astype(BF16)
        ugrad[:, lanes] = (hg * g * s).astype(BF16)

    grads = ((ggrad, tok, wg), (ugrad, tok, wu), (hid, cot, wd))
    strip = 256 if width % 256 == 0 else width
    strips = width // strip - left_over(width // strip)

    def grad_strip(n, carry):
        cols = pl.ds(pl.multiple_of(n * strip, strip), strip)
        for left, right, out in grads:
            r = right[:, :, :, cols].reshape(experts * pad, strip)
            out[:, cols] = jnp.dot(left[...], r, preferred_element_type=F32).astype(BF16)
        return carry

    def bcopy(j, r, h):
        cols = pl.ds(h * piece, piece)
        return remote(
            back.at[j, r, 0 : sizes[j], cols], plane_in.at[j, q, 0 : sizes[j], cols],
            bsend.at[min(j, 1)], brecv.at[j, h],
            (z * PLANE + mates[r], c),
        )

    def give(j):
        size = sizes[j]
        vcopy(j).wait_recv()
        for h in range(PARTS):
            cols = pl.ds(h * piece, piece)
            spot = pl.ds(pl.multiple_of(c * half + h * piece, piece), piece)
            for r in (2, 0, 1, 3):
                m = mates[r] if r < 3 else q
                total = (
                    val[j, m, 0:size, spot].astype(F32) + partner_in[j, m, 0:size, cols].astype(F32)
                ).astype(BF16)
                if r < 3:
                    back[j, r, 0:size, cols] = total
                    bcopy(j, r, h).start()
                else:
                    plane_in[j, q, 0:size, cols] = total

    def mixing(j):
        blk = seq[j]
        weights, takes = [], []
        for m in range(PLANE):
            e = z * PLANE + m
            rank = side_ref[blk, pl.ds(e, 1), :]
            strength = side_ref[blk, pl.ds(experts + e, 1), :]
            spots = [(j, sizes[j])] + ([(j + 1, 16)] if j + 1 < LINE else [])
            for i, size in spots:
                base = float(offs[i] - capacity * j)
                w = jnp.where(slot_id[:size] + base == rank, strength, 0.0)
                high = w.astype(BF16)
                weights += [high, (w - high.astype(F32)).astype(BF16)]
                takes += [(i, m, size)] * 2
        return jnp.concatenate(weights, axis=0), takes

    def combine(j, h, mix):
        weights, takes = mix
        cols = pl.ds(h * piece, piece)
        remote(
            back.at[j, :, 0 : sizes[j], cols], plane_in.at[j, 0:3, 0 : sizes[j], cols],
            bsend.at[min(j, 1)], brecv.at[j, h], partner,
        ).wait_recv()
        values = jnp.concatenate([plane_in[i, m, 0:size, cols] for i, m, size in takes], axis=0)
        acc[seq[j], :, cols] = lax.dot_general(weights, values, tn, preferred_element_type=F32)

    def ucopy(w, s, h):
        cols = pl.ds(h * piece, piece)
        to = d + (2 * w - 1) * PLANE
        return remote(
            out_stage.at[w, s, :, cols], line_in.at[w, s, :, cols], usend.at[w],
            urecv.at[w, s, h], (to, c),
        )

    def height(w):
        return z if w == 1 else LINE - 1 - z

    def lifts(w, s):
        return (height(w) <= s) & (height(w) < LINE - 1)

    def lands(w, s):
        return (height(w) > 0) & (height(w) - 1 <= s)

    def lift(s, h):
        cols = pl.ds(h * piece, piece)
        for w in (1, 0):
            blk = z + (2 * w - 1) * (LINE - 1 - s)
            if s > 0:
                @pl.when(lands(w, s - 1))
                def _():
                    ucopy(w, s - 1, h).wait_recv()

                @pl.when(lifts(w, s) & (height(w) > 0))
                def _():
                    out_stage[w, s, :, cols] = (
                        acc[blk, :, cols] + line_in[w, s - 1, :, cols].astype(F32)
                    ).astype(BF16)
                    ucopy(w, s, h).start()

            @pl.when(lifts(w, s) & (height(w) == 0))
            def _():
                out_stage[w, s, :, cols] = acc[blk, :, cols].astype(BF16)
                ucopy(w, s, h).start()

    def sides():
        expert_id = lax.broadcasted_iota(jnp.int32, (experts, sel_rows), 0)
        member = jnp.zeros((experts, sel_rows), F32)
        gate = jnp.zeros((experts, sel_rows), F32)
        for k in range(top):
            eq = rt_ref[k : k + 1, :] == expert_id
            member = member + jnp.where(eq, 1.0, 0.0)
            gate = gate + jnp.where(eq, gt_ref[k : k + 1, :], 0.0)
        tri = jnp.where(
            lax.broadcasted_iota(jnp.int32, (sel_rows, sel_rows), 0)
            < lax.broadcasted_iota(jnp.int32, (sel_rows, sel_rows), 1),
            1.0,
            0.0,
        ).astype(BF16)
        before = jnp.dot(member.astype(BF16), tri, preferred_element_type=F32)
        side_ref[z, 0:experts, :] = jnp.where(member > 0.5, before, -1024.0)
        side_ref[z, experts : 2 * experts, :] = gate

    def rewards():
        rw = rw_ref[...].astype(F32)
        rw_rows = jnp.concatenate(
            [jnp.broadcast_to(rw[i : i + 1, :], (16, rw.shape[1])) for i in range(rw.shape[0])],
            axis=1,
        ).astype(BF16)
        part[...] = lax.dot_general(rw_rows, data[0, z], nt, preferred_element_type=F32)

    reward_copy = remote(part, part_in, psend, precv, partner)
    greeted(z)
    zstart(0, 0, (1,))
    for cp in loads[6:9]:
        cp.start()
    loads[2].wait()
    loads[3].wait()
    sides()
    zstart(0, 0, (0,))
    loads[5].wait()
    zstart(1, 0, (1,), "outer")
    pick(0, 0)
    loads[4].wait()
    rewards()
    reward_copy.start()
    for j in range(LINE):
        if sizes[j] < pad:
            for a in (0, 1):
                rows[a][j, :, sizes[j] : pad, :] = jnp.zeros(
                    (PLANE, pad - sizes[j], width), BF16
                )
    reward_copy.wait()
    scale[z] = sigmoid(part[0:1, :] + part_in[0:1, :]) * side_ref[z, experts : 2 * experts, :]
    zstart(1, 0, (0,))
    pick(1, 0)
    forward(0, 0)
    zwait(0, 0)
    zstart(0, 1)
    zstart(1, 0, (1,), "inner")
    pick(0, 1)
    for cp in loads[6:9]:
        cp.wait()
    group(0)
    forward(1, 0)
    zwait(1, 0, "outer")
    pick(1, 1)
    grad_group(0)
    forward(0, 1)
    zwait(0, 1)
    zstart(0, 2)
    zstart(1, 1, links="inner")
    pick(0, 2)
    group(1)
    forward(1, 1)
    zwait(1, 0, "inner")
    zstart(1, 1, links="outer")
    zwait(0, 2)
    pick(0, 3)
    grad_group(1)
    forward(0, 2)
    zwait(1, 1)
    zstart(1, 2)
    pick(1, 2)
    group(2)
    forward(0, 3)
    zwait(1, 2)
    pick(1, 3)
    group(3)
    for j in (3, 2, 1, 0):
        give(j)
    forward(1, 2)
    grad_group(2)
    forward(1, 3)
    grad_group(3)

    last = LINE - 2
    turns = (LINE - 1) * PARTS
    done, turn = 0, 0
    for s in range(LINE - 1):
        j = LINE - 1 - s
        mix = mixing(j)
        for h in range(PARTS):
            combine(j, h, mix)
            lift(s, h)
            upto = strips * turn // (turns - 2)
            upto = min(upto, strips)
            if upto > done:
                lax.fori_loop(done, upto, grad_strip, 0)
                done = upto
            turn = turn + 1
    lax.fori_loop(done, strips, grad_strip, 0)

    def sent(src, sem):
        remote(src, src, sem, vrecv.at[0], partner).wait_send()

    for w in (0, 1):
        for n in range(1, LINE):
            @pl.when(LINE - height(1 - w) == n)
            def _():
                sent(data.at[:, 0:n], zsend.at[w])
                sent(side_ref.at[0:n], ssend.at[w])
                sent(scale.at[0:n], csend.at[w])
    for i, cut in ((0, slice(0, 1)), (1, slice(1, LINE))):
        size = sizes[0] if i == 0 else pad
        sent(stage.at[:, cut, :, 0:size, :], xsend.at[i])
        sent(val.at[cut, :, 0:size, other], vsend.at[i])
        for a in (0, 1):
            sent(rows[a].at[cut, :, 0:size, mine], tsend.at[a, i])

    mix = mixing(0)
    for h in range(PARTS):
        combine(0, h, mix)
        cols = pl.ds(h * piece, piece)
        for w in (1, 0):
            @pl.when(lands(w, last))
            def _():
                ucopy(w, last, h).wait_recv()
                acc[z, :, cols] = acc[z, :, cols] + line_in[w, last, :, cols].astype(F32)
        mixed_ref[:, cols] = acc[z, :, cols].astype(BF16)

    for w in (0, 1):
        for n in range(1, LINE):
            @pl.when(LINE - 1 - height(w) == n)
            def _():
                sent(out_stage.at[w, 0:n], usend.at[w])
    sent(back.at[0:1, :, 0 : sizes[0], :], bsend.at[0])
    sent(back.at[1:LINE], bsend.at[1])


def left_over(strips):
    return strips // 4


def flush_kernel(
    mixed, gg, gu, gd, tok, cot, hid, ggrad, ugrad, mixed_out, gg_out, gu_out, gd_out, last, sem
):
    units, width = gg.shape[1:]
    late = last.shape[1] * last.shape[3]
    strip = last.shape[3]
    early = width - late
    rows = units // PARTS
    copies = [pltpu.make_async_copy(mixed, mixed_out, sem.at[0, 0])]
    grads = ((gg, gg_out, ggrad, tok), (gu, gu_out, ugrad, tok), (gd, gd_out, hid, cot))
    for i, (src, dst, _, _) in enumerate(grads):
        for p in range(PARTS):
            at = (0, pl.ds(p * rows, rows), pl.ds(0, early))
            copies.append(pltpu.make_async_copy(src.at[at], dst.at[at], sem.at[i + 1, p]))
    for cp in copies:
        cp.start()
    for n in range(last.shape[1]):
        cols = pl.ds(early + n * strip, strip)
        for i, (_, dst, left, right) in enumerate(grads):
            r = right[:, :, :, cols].reshape(left.shape[1], strip)
            last[i, n] = jnp.dot(left[...], r, preferred_element_type=F32).astype(BF16)
            cp = pltpu.make_async_copy(last.at[i, n], dst.at[0, :, cols], sem.at[i + 1, PARTS + n])
            cp.start()
            copies.append(cp)
    for cp in copies:
        cp.wait()


def flush(*outs):
    units, width = outs[1].shape[1:]
    strip = 256 if width % 256 == 0 else width
    late = left_over(width // strip)
    return pl.pallas_call(
        flush_kernel,
        name="flush",
        out_shape=tuple(jax.ShapeDtypeStruct(o.shape, o.dtype) for o in outs[:4]),
        in_specs=vmem(len(outs)),
        out_specs=tuple(hbm(4)),
        scratch_shapes=[pltpu.VMEM((3, late, units, strip), BF16), DMA((4, PARTS + late))],
        compiler_params=pltpu.CompilerParams(vmem_limit_bytes=12 << 20),
    )(*[pltpu.with_memory_space_constraint(o, pltpu.VMEM) for o in outs])


def vmem(count):
    return [pl.BlockSpec(memory_space=pltpu.VMEM)] * count


def hbm(count):
    return [pl.BlockSpec(memory_space=pl.ANY)] * count


DMA = pltpu.SemaphoreType.DMA


def planar(pool, select, reward_w, routes, gates, target, w_gate, w_up, w_down):
    experts = LINE * PLANE
    sel_rows, top = routes.shape
    capacity = 5 * sel_rows * top // (4 * experts)
    pad = max(chunks(capacity)[1])
    half = target.shape[1]
    units, width = w_gate.shape[1:]
    span = PLANE * pad
    grad_shape = pltpu.VMEM(w_gate.shape, BF16)
    rw = reward_w.reshape(half // 128, 128)
    slots = pltpu.VMEM((LINE, PLANE, pad, width), BF16)
    act = pltpu.VMEM((LINE, units, span), F32)
    flat = pltpu.VMEM((units, experts * pad), BF16)
    outs = pl.pallas_call(
        functools.partial(layer_kernel, capacity, pad),
        name="layer",
        out_shape=(
            pltpu.VMEM((sel_rows, half), BF16), grad_shape, grad_shape, grad_shape,
            slots, slots, flat, flat, flat,
        ),
        in_specs=hbm(9),
        out_specs=tuple(vmem(9)),
        scratch_shapes=[
            pltpu.VMEM(pool.shape, BF16), pltpu.VMEM((1, sel_rows), jnp.int32),
            pltpu.VMEM(rw.shape, BF16), pltpu.VMEM((top, sel_rows), jnp.int32),
            pltpu.VMEM((top, sel_rows), F32), act, act, slots,
            pltpu.VMEM((2, LINE, sel_rows, half), BF16),
            pltpu.VMEM((LINE, 2 * experts, sel_rows), F32),
            pltpu.VMEM((LINE, experts, sel_rows), F32),
            pltpu.VMEM((16, sel_rows), F32),
            pltpu.VMEM((16, sel_rows), F32),
            pltpu.VMEM((2, LINE, 3, pad, half), BF16),
            pltpu.VMEM((LINE, PLANE, pad, half), BF16),
            pltpu.VMEM((LINE, 3, pad, half), BF16),
            pltpu.VMEM((LINE, PLANE, pad, half), BF16),
            pltpu.VMEM((LINE, sel_rows, half), F32),
            pltpu.VMEM((2, LINE - 1, sel_rows, half), BF16),
            pltpu.VMEM((2, LINE - 1, sel_rows, half), BF16),
            DMA((9,)),
            DMA((2,)), DMA((2, LINE)), DMA((2,)), DMA((LINE,)),
            DMA((2,)), DMA((LINE,)), DMA((2,)), DMA((2, LINE)),
            DMA((2, 2)), DMA((2, LINE)), DMA, DMA,
            DMA((2,)), DMA((LINE,)), DMA((2,)), DMA((LINE, PARTS)),
            DMA((2,)), DMA((2, LINE - 1, PARTS)),
        ],
        compiler_params=pltpu.CompilerParams(
            collective_id=0, has_side_effects=True, vmem_limit_bytes=44 * 10**6
        ),
    )(pool, select.reshape(1, sel_rows), rw, routes.T, gates.T, target,
      w_gate, w_up, w_down)
    return flush(*outs)


def solution(mesh):
    in_specs = (
        P("dp", "tensor"), P("dp"), P("tensor"), P("dp", None), P("dp", None), P("dp", "tensor"),
        P("dp", "tensor", None), P("dp", "tensor", None), P("dp", "tensor", None),
    )
    out_specs = (
        P("dp", "tensor"), P("dp", "tensor", None), P("dp", "tensor", None),
        P("dp", "tensor", None),
    )
    dp, tensor = mesh.shape["dp"], mesh.shape["tensor"]
    fits = tensor == 2 and dp == LINE * PLANE
    local = planar if fits else generic
    return jax.shard_map(local, mesh=mesh, in_specs=in_specs, out_specs=out_specs, check_vma=False)
```

```python
import functools
import jax
import jax.numpy as jnp
from jax import lax
from jax.experimental import pallas as pl
from jax.experimental.pallas import tpu as pltpu
from jax.sharding import PartitionSpec as P

MESH = pl.DeviceIdType.MESH
PLANE = 4
LINE = 4
PARTS = 2
F32 = jnp.float32
BF16 = jnp.bfloat16


def slot_factor(route_hit, weights):
    return jnp.sum(jnp.where(route_hit, weights.reshape(-1)[:, None], 0.0), axis=0)


def generic(pool, select, reward_w, routes, gates, target, w_gate, w_up, w_down):
    pool_rows = pool.shape[0]
    local_rows = select - lax.axis_index("dp") * pool_rows
    chosen = jnp.take(pool, local_rows, axis=0)
    sel_rows, top_count = routes.shape
    owners = lax.axis_size("dp")
    exp_dev = w_gate.shape[0]
    experts = owners * exp_dev
    capacity = 5 * sel_rows * top_count // (4 * experts)
    slot_count = experts * capacity
    flat_routes = routes.reshape(-1)
    onehot = (flat_routes[:, None] == jnp.arange(experts, dtype=jnp.int32)[None, :]).astype(
        jnp.int32
    )
    before = jnp.cumsum(onehot, axis=0) - onehot
    slot_rank = jnp.sum(before * onehot, axis=1)
    slot_place = flat_routes * capacity + slot_rank
    route_hit = slot_place[:, None] == jnp.arange(slot_count, dtype=jnp.int32)[None, :]
    route_pick = route_hit.astype(jnp.bfloat16).reshape(sel_rows, top_count, slot_count)
    token_pick = jnp.sum(route_pick, axis=1)
    reward = lax.psum(jnp.dot(chosen, reward_w, preferred_element_type=jnp.float32), "tensor")
    keep_scale = jax.nn.sigmoid(reward)
    slot_scale = slot_factor(route_hit, keep_scale[:, None] * gates)
    token_send = jnp.einsum(
        "sp,sd->pd", token_pick, chosen, preferred_element_type=jnp.float32
    ).astype(jnp.bfloat16)
    picked_target = jnp.einsum("sp,sd->pd", token_pick, target, preferred_element_type=jnp.float32)
    cot_send = (picked_target * slot_scale[:, None]).astype(jnp.bfloat16)
    token_part, cot_part = (
        lax.all_to_all(token_send, "dp", split_axis=0, concat_axis=0, tiled=True),
        lax.all_to_all(cot_send, "dp", split_axis=0, concat_axis=0, tiled=True),
    )
    received_tokens, received_cots = (
        lax.all_gather(token_part, "tensor", axis=1, tiled=True),
        lax.all_gather(cot_part, "tensor", axis=1, tiled=True),
    )
    width = received_tokens.shape[1]
    token_rows = received_tokens.reshape(owners, exp_dev, capacity, width)
    cot_rows = received_cots.reshape(owners, exp_dev, capacity, width)
    gate_act = jnp.einsum("secd,efd->secf", token_rows, w_gate, preferred_element_type=jnp.float32)
    up_act = jnp.einsum("secd,efd->secf", token_rows, w_up, preferred_element_type=jnp.float32)
    sigmoid_gate = jax.nn.sigmoid(gate_act)
    hidden = (gate_act * sigmoid_gate * up_act).astype(jnp.bfloat16)
    partial_value = jnp.einsum("secf,efd->secd", hidden, w_down, preferred_element_type=jnp.float32)
    summed = lax.psum_scatter(
        partial_value.astype(jnp.bfloat16), "tensor", scatter_dimension=3, tiled=True
    )
    returned = lax.all_to_all(summed, "dp", split_axis=0, concat_axis=0, tiled=True).reshape(
        slot_count, -1
    )
    route_rows = jnp.einsum("skp,pd->skd", route_pick, returned, preferred_element_type=jnp.float32)
    mixed = jnp.sum(route_rows * gates[:, :, None], axis=1).astype(jnp.bfloat16)
    hidden_grad = jnp.einsum("secd,efd->secf", cot_rows, w_down, preferred_element_type=jnp.float32)
    gate_grad = (
        hidden_grad * up_act * sigmoid_gate * (1.0 + gate_act * (1.0 - sigmoid_gate))
    ).astype(jnp.bfloat16)
    up_grad = (hidden_grad * gate_act * sigmoid_gate).astype(jnp.bfloat16)
    grad_down = jnp.einsum(
        "secf,secd->efd", hidden, cot_rows, preferred_element_type=jnp.float32
    ).astype(jnp.bfloat16)
    grad_gate = jnp.einsum(
        "secf,secd->efd", gate_grad, token_rows, preferred_element_type=jnp.float32
    ).astype(jnp.bfloat16)
    grad_up = jnp.einsum(
        "secf,secd->efd", up_grad, token_rows, preferred_element_type=jnp.float32
    ).astype(jnp.bfloat16)
    return (mixed, grad_gate, grad_up, grad_down)


def place():
    d = lax.axis_index("dp")
    c = lax.axis_index("tensor")
    z, q = d // PLANE, d % PLANE
    y, x = q // 2, q % 2
    mates = [((y + ry) % 2) * 2 + (x + rx) % 2 for ry, rx in ((0, 1), (1, 0), (1, 1))]
    return d, c, z, q, mates


def greet(d, c, z, q, mates):
    barrier = pltpu.get_barrier_semaphore()
    for m in mates:
        pl.semaphore_signal(barrier, inc=1, device_id=(z * PLANE + m, c), device_id_type=MESH)
    pl.semaphore_signal(barrier, inc=1, device_id=(d, 1 - c), device_id_type=MESH)

    @pl.when(z > 0)
    def _():
        pl.semaphore_signal(barrier, inc=1, device_id=(d - PLANE, c), device_id_type=MESH)

    @pl.when(z < LINE - 1)
    def _():
        pl.semaphore_signal(barrier, inc=1, device_id=(d + PLANE, c), device_id_type=MESH)


def greeted(z):
    below, above = (z + LINE - 1) // LINE, (2 * LINE - 2 - z) // LINE
    pl.semaphore_wait(pltpu.get_barrier_semaphore(), 4 + below + above)


def remote(src, dst, send, recv, dev):
    return pltpu.make_async_remote_copy(
        src_ref=src, dst_ref=dst, send_sem=send, recv_sem=recv, device_id=dev, device_id_type=MESH
    )


def sigmoid(v):
    return 1.0 / (1.0 + jnp.exp(-v))


def chunks(capacity):
    ends = [(j + 1) * capacity // 16 * 16 for j in range(LINE - 1)]
    ends.append(-(-LINE * capacity // 16) * 16)
    offs = [0] + ends[:-1]
    return offs, [b - a for a, b in zip(offs, ends)]


def layer_kernel(
    capacity, pad, pool_hbm, sel_hbm, rw_hbm, rt_hbm, gt_hbm, target_hbm, wg_hbm, wu_hbm, wd_hbm,
    mixed_ref, gg_ref, gu_ref, gd_ref, tok, cot, hid, ggrad, ugrad,
    pool_ref, sel_ref, rw_ref, rt_ref, gt_ref, gate_act, up_act, val,
    data, side_ref, scale, part, part_in, stage,
    partner_in, back, plane_in, acc, out_stage, line_in,
    lsem, zsend, zrecv, ssend, srecv, csend, crecv, xsend, xrecv, tsend, trecv, psend, precv,
    vsend, vrecv, bsend, brecv, usend, urecv,
):
    d, c, z, q, mates = place()
    experts = LINE * PLANE
    sel_rows, half = mixed_ref.shape
    top = gt_hbm.shape[0]
    wg, wu, wd = gg_ref.at[0], gu_ref.at[0], gd_ref.at[0]
    units, width = wg.shape
    span = PLANE * pad
    offs, sizes = chunks(capacity)
    rows = (tok, cot)
    mine = pl.ds(pl.multiple_of(c * half, half), half)
    other = pl.ds(pl.multiple_of((1 - c) * half, half), half)
    partner = (d, 1 - c)
    seq = (z, z + 1 - 2 * (z % 2), 2 - z // 2, 3 - 3 * (z // 2))
    piece = half // PARTS
    nt = (((1,), (1,)), ((), ()))
    tn = (((0,), (0,)), ((), ()))

    greet(d, c, z, q, mates)
    loads = [
        pltpu.make_async_copy(src, dst, lsem.at[i])
        for i, (src, dst) in enumerate((
            (sel_hbm, sel_ref), (pool_hbm, pool_ref), (rt_hbm, rt_ref), (gt_hbm, gt_ref),
            (rw_hbm, rw_ref), (target_hbm, data.at[1, z]), (wg_hbm.at[0], wg), (wu_hbm.at[0], wu),
            (wd_hbm.at[0], wd),
        ))
    ]
    for i in (0, 2, 3, 1, 4):
        loads[i].start()

    def sides():
        expert_id = lax.broadcasted_iota(jnp.int32, (experts, sel_rows), 0)
        member = jnp.zeros((experts, sel_rows), F32)
        gate = jnp.zeros((experts, sel_rows), F32)
        for k in range(top):
            eq = rt_ref[k : k + 1, :] == expert_id
            member = member + jnp.where(eq, 1.0, 0.0)
            gate = gate + jnp.where(eq, gt_ref[k : k + 1, :], 0.0)
        tri = jnp.where(
            lax.broadcasted_iota(jnp.int32, (sel_rows, sel_rows), 0)
            < lax.broadcasted_iota(jnp.int32, (sel_rows, sel_rows), 1),
            1.0,
            0.0,
        ).astype(BF16)
        before = jnp.dot(member.astype(BF16), tri, preferred_element_type=F32)
        side_ref[z, 0:experts, :] = jnp.where(member > 0.5, before, -1024.0)
        side_ref[z, experts : 2 * experts, :] = gate

    loads[0].wait()
    pool_rows = pool_ref.shape[0]
    hit = (
        lax.broadcasted_iota(jnp.int32, (pool_rows, sel_rows), 0) == sel_ref[...] - d * pool_rows
    ).astype(F32).astype(BF16)
    loads[2].wait()
    loads[3].wait()
    sides()
    loads[1].wait()
    loads[5].start()
    chosen = lax.dot_general(
        hit, pool_ref[...], tn, preferred_element_type=F32
    ).astype(BF16)
    data[0, z] = chosen

    def zcopy(a, s, way, kind):
        blk = z - way * s
        dev = (d + way * PLANE, c)
        w = (way + 1) // 2
        if kind == 1:
            spot = data.at[a, blk]
            return remote(spot, spot, zsend.at[w], zrecv.at[a, blk], dev)
        if a == 0:
            spot = side_ref.at[blk]
            return remote(spot, spot, ssend.at[w], srecv.at[blk], dev)
        spot = scale.at[blk]
        return remote(spot, spot, csend.at[w], crecv.at[blk], dev)

    def inside(to):
        return (z > 0) & (z < LINE - 1) & (to > 0) & (to < LINE - 1)

    def among(links, to):
        return {"all": True, "inner": inside(to), "outer": jnp.logical_not(inside(to))}[links]

    def sends(s, way):
        blk, to = z - way * s, z + way
        return (blk >= 0) & (blk < LINE) & (to >= 0) & (to < LINE)

    def zstart(a, s, which=(0, 1), links="all"):
        for way in (1, -1):
            @pl.when(sends(s, way) & among(links, z + way))
            def _():
                for i in which:
                    zcopy(a, s, way, i).start()

    def arrives(s, way):
        blk = z - way * (s + 1)
        return (blk >= 0) & (blk < LINE)

    def zwait(a, s, links="all"):
        for way in (1, -1):
            @pl.when(arrives(s, way) & among(links, z - way))
            def _():
                blk = z - way * (s + 1)
                remote(
                    data.at[a, blk], data.at[a, blk], zsend.at[0], zrecv.at[a, blk], partner
                ).wait_recv()
                if a == 0:
                    remote(
                        side_ref.at[blk], side_ref.at[blk], ssend.at[0], srecv.at[blk], partner
                    ).wait_recv()
                else:
                    remote(
                        scale.at[blk], scale.at[blk], csend.at[0], crecv.at[blk], partner
                    ).wait_recv()

    def tcopy(a, j, m):
        spot = rows[a].at[j, m, 0 : sizes[j], mine]
        return remote(spot, spot, tsend.at[a, min(j, 1)], trecv.at[a, j], partner)

    def tall(a, j, side):
        spot = rows[a].at[j, :, 0 : sizes[j], side]
        return remote(spot, spot, tsend.at[a, min(j, 1)], trecv.at[a, j], partner)

    def tarrive(a, j):
        tall(a, j, other).wait_recv()

    def xcopy(a, j, r):
        return remote(
            stage.at[a, j, r, 0 : sizes[j], :],
            rows[a].at[j, q, 0 : sizes[j], mine],
            xsend.at[min(j, 1)],
            xrecv.at[a, j],
            (z * PLANE + mates[r], c),
        )

    slot_id = lax.broadcasted_iota(jnp.int32, (pad, sel_rows), 0).astype(F32)

    def pick(a, j):
        size = sizes[j]
        sources = [(seq[i], float(offs[j] - capacity * i)) for i in ((j, j - 1) if j else (j,))]
        sides = (2, 0, 1, 3)
        hits, factors = [], []
        for r in sides:
            e = z * PLANE + (mates[r] if r < 3 else q)
            ms = [slot_id[:size] + base == side_ref[b, pl.ds(e, 1), :] for b, base in sources]
            hits.append(jnp.concatenate([jnp.where(m, 1.0, 0.0) for m in ms], axis=1))
            if a == 1:
                total = sum(
                    jnp.where(m, scale[b, pl.ds(e, 1), :], 0.0) for m, (b, _) in zip(ms, sources)
                )
                factors.append(jnp.sum(total, axis=1, keepdims=True))
        hits = jnp.concatenate(hits, axis=0).astype(BF16)
        if a == 1:
            factors = jnp.concatenate(factors, axis=0)
        cut = 256 if half % 256 == 0 else half
        for n in range(half // cut):
            cols = pl.ds(n * cut, cut)
            source = jnp.concatenate([data[a, b, :, cols] for b, _ in sources], axis=0)
            picked = jnp.dot(hits, source, preferred_element_type=F32)
            if a == 1:
                picked = picked * factors
            picked = picked.astype(BF16)
            for i, r in enumerate(sides):
                got = picked[i * size : (i + 1) * size]
                if r < 3:
                    stage[a, j, r, 0:size, cols] = got
                else:
                    spot = pl.ds(pl.multiple_of(c * half + n * cut, cut), cut)
                    rows[a][j, q, 0:size, spot] = got
        for r in (2, 0, 1):
            xcopy(a, j, r).start()
        tcopy(a, j, q).start()

    def forward(a, j):
        remote(
            stage.at[a, j, :, 0 : sizes[j], :], rows[a].at[j, 0:3, 0 : sizes[j], mine],
            xsend.at[min(j, 1)], xrecv.at[a, j], partner,
        ).wait_recv()
        for m in mates:
            tcopy(a, j, m).start()

    def vcopy(j):
        return remote(
            val.at[j, :, 0 : sizes[j], other], partner_in.at[j, :, 0 : sizes[j], :],
            vsend.at[min(j, 1)], vrecv.at[j], partner,
        )

    tile = 512 if half % 512 == 0 else half

    def group(j):
        lanes = pl.ds(j * span, span)
        tarrive(0, j)
        x = tok[j].reshape(span, width)
        g = lax.dot_general(wg[...], x, nt, preferred_element_type=F32)
        u = lax.dot_general(wu[...], x, nt, preferred_element_type=F32)
        gate_act[j] = g
        up_act[j] = u
        h = (g * sigmoid(g) * u).astype(BF16)
        hid[:, lanes] = h
        for side in (1 - c, c):
            for n in range(half // tile):
                cols = pl.ds(pl.multiple_of(side * half + n * tile, tile), tile)
                v = lax.dot_general(h, wd[:, cols], tn, preferred_element_type=F32)
                val[j, :, :, cols] = v.astype(BF16).reshape(PLANE, pad, tile)
            if side is not c:
                vcopy(j).start()

    def grad_group(j):
        lanes = pl.ds(j * span, span)
        tarrive(1, j)
        x = cot[j].reshape(span, width)
        hg = lax.dot_general(wd[...], x, nt, preferred_element_type=F32)
        g = gate_act[j]
        s = sigmoid(g)
        ggrad[:, lanes] = (hg * up_act[j] * s * (1.0 + g * (1.0 - s))).astype(BF16)
        ugrad[:, lanes] = (hg * g * s).astype(BF16)

    grads = ((ggrad, tok, wg), (ugrad, tok, wu), (hid, cot, wd))
    strip = 256 if width % 256 == 0 else width
    strips = width // strip - left_over(width // strip)

    def grad_strip(n, carry):
        cols = pl.ds(pl.multiple_of(n * strip, strip), strip)
        for left, right, out in grads:
            r = right[:, :, :, cols].reshape(experts * pad, strip)
            out[:, cols] = jnp.dot(left[...], r, preferred_element_type=F32).astype(BF16)
        return carry

    def bcopy(j, r, h):
        cols = pl.ds(h * piece, piece)
        return remote(
            back.at[j, r, 0 : sizes[j], cols], plane_in.at[j, q, 0 : sizes[j], cols],
            bsend.at[min(j, 1)], brecv.at[j, h],
            (z * PLANE + mates[r], c),
        )

    def give(j):
        size = sizes[j]
        vcopy(j).wait_recv()
        for h in range(PARTS):
            cols = pl.ds(h * piece, piece)
            spot = pl.ds(pl.multiple_of(c * half + h * piece, piece), piece)
            for r in (2, 0, 1, 3):
                m = mates[r] if r < 3 else q
                total = (
                    val[j, m, 0:size, spot].astype(F32) + partner_in[j, m, 0:size, cols].astype(F32)
                ).astype(BF16)
                if r < 3:
                    back[j, r, 0:size, cols] = total
                    bcopy(j, r, h).start()
                else:
                    plane_in[j, q, 0:size, cols] = total

    def mixing(j):
        blk = seq[j]
        weights, takes = [], []
        for m in range(PLANE):
            e = z * PLANE + m
            rank = side_ref[blk, pl.ds(e, 1), :]
            strength = side_ref[blk, pl.ds(experts + e, 1), :]
            spots = [(j, sizes[j])] + ([(j + 1, 16)] if j + 1 < LINE else [])
            for i, size in spots:
                base = float(offs[i] - capacity * j)
                w = jnp.where(slot_id[:size] + base == rank, strength, 0.0)
                high = w.astype(BF16)
                weights += [high, (w - high.astype(F32)).astype(BF16)]
                takes += [(i, m, size)] * 2
        return jnp.concatenate(weights, axis=0), takes

    def combine(j, h, mix):
        weights, takes = mix
        cols = pl.ds(h * piece, piece)
        remote(
            back.at[j, :, 0 : sizes[j], cols], plane_in.at[j, 0:3, 0 : sizes[j], cols],
            bsend.at[min(j, 1)], brecv.at[j, h], partner,
        ).wait_recv()
        values = jnp.concatenate([plane_in[i, m, 0:size, cols] for i, m, size in takes], axis=0)
        acc[seq[j], :, cols] = lax.dot_general(weights, values, tn, preferred_element_type=F32)

    def ucopy(w, s, h):
        cols = pl.ds(h * piece, piece)
        to = d + (2 * w - 1) * PLANE
        return remote(
            out_stage.at[w, s, :, cols], line_in.at[w, s, :, cols], usend.at[w],
            urecv.at[w, s, h], (to, c),
        )

    def height(w):
        return z if w == 1 else LINE - 1 - z

    def lifts(w, s):
        return (height(w) <= s) & (height(w) < LINE - 1)

    def lands(w, s):
        return (height(w) > 0) & (height(w) - 1 <= s)

    def lift(s, h):
        cols = pl.ds(h * piece, piece)
        for w in (1, 0):
            blk = z + (2 * w - 1) * (LINE - 1 - s)
            if s > 0:
                @pl.when(lands(w, s - 1))
                def _():
                    ucopy(w, s - 1, h).wait_recv()

                @pl.when(lifts(w, s) & (height(w) > 0))
                def _():
                    out_stage[w, s, :, cols] = (
                        acc[blk, :, cols] + line_in[w, s - 1, :, cols].astype(F32)
                    ).astype(BF16)
                    ucopy(w, s, h).start()

            @pl.when(lifts(w, s) & (height(w) == 0))
            def _():
                out_stage[w, s, :, cols] = acc[blk, :, cols].astype(BF16)
                ucopy(w, s, h).start()

    def rewards():
        rw = rw_ref[...].astype(F32)
        rw_rows = jnp.concatenate(
            [jnp.broadcast_to(rw[i : i + 1, :], (16, rw.shape[1])) for i in range(rw.shape[0])],
            axis=1,
        ).astype(BF16)
        part[...] = lax.dot_general(rw_rows, data[0, z], nt, preferred_element_type=F32)

    reward_copy = remote(part, part_in, psend, precv, partner)
    greeted(z)
    zstart(0, 0, (1,))
    zstart(0, 0, (0,))
    pick(0, 0)
    loads[5].wait()
    zstart(1, 0, (1,), "outer")
    for cp in loads[6:9]:
        cp.start()
    loads[4].wait()
    rewards()
    reward_copy.start()
    for j in range(LINE):
        if sizes[j] < pad:
            for a in (0, 1):
                rows[a][j, :, sizes[j] : pad, :] = jnp.zeros(
                    (PLANE, pad - sizes[j], width), BF16
                )
    reward_copy.wait()
    scale[z] = sigmoid(part[0:1, :] + part_in[0:1, :]) * side_ref[z, experts : 2 * experts, :]
    zstart(1, 0, (0,))
    pick(1, 0)
    forward(0, 0)
    zwait(0, 0)
    zstart(0, 1)
    zstart(1, 0, (1,), "inner")
    pick(0, 1)
    for cp in loads[6:9]:
        cp.wait()
    group(0)
    forward(1, 0)
    zwait(1, 0, "outer")
    pick(1, 1)
    grad_group(0)
    forward(0, 1)
    zwait(0, 1)
    zstart(0, 2)
    zstart(1, 1, links="inner")
    pick(0, 2)
    group(1)
    forward(1, 1)
    zwait(1, 0, "inner")
    zstart(1, 1, links="outer")
    zwait(0, 2)
    pick(0, 3)
    grad_group(1)
    forward(0, 2)
    zwait(1, 1)
    zstart(1, 2)
    pick(1, 2)
    group(2)
    forward(0, 3)
    zwait(1, 2)
    pick(1, 3)
    group(3)
    for j in (3, 2, 1, 0):
        give(j)
    forward(1, 2)
    grad_group(2)
    forward(1, 3)
    grad_group(3)

    last = LINE - 2
    done, turn = 0, 0
    for s in range(LINE - 1):
        j = LINE - 1 - s
        mix = mixing(j)
        for h in range(PARTS):
            combine(j, h, mix)
            lift(s, h)
            upto = min(2 * turn + 1, strips)
            if upto > done:
                lax.fori_loop(done, upto, grad_strip, 0)
                done = upto
            turn = turn + 1
    lax.fori_loop(done, strips, grad_strip, 0)

    def sent(src, sem):
        remote(src, src, sem, vrecv.at[0], partner).wait_send()

    for w in (0, 1):
        for n in range(1, LINE):
            @pl.when(LINE - height(1 - w) == n)
            def _():
                sent(data.at[:, 0:n], zsend.at[w])
                sent(side_ref.at[0:n], ssend.at[w])
                sent(scale.at[0:n], csend.at[w])
    for i, cut in ((0, slice(0, 1)), (1, slice(1, LINE))):
        size = sizes[0] if i == 0 else pad
        sent(stage.at[:, cut, :, 0:size, :], xsend.at[i])
        sent(val.at[cut, :, 0:size, other], vsend.at[i])
        for a in (0, 1):
            sent(rows[a].at[cut, :, 0:size, mine], tsend.at[a, i])

    mix = mixing(0)
    for h in range(PARTS):
        combine(0, h, mix)
        cols = pl.ds(h * piece, piece)
        for w in (1, 0):
            @pl.when(lands(w, last))
            def _():
                ucopy(w, last, h).wait_recv()
                acc[z, :, cols] = acc[z, :, cols] + line_in[w, last, :, cols].astype(F32)
        mixed_ref[:, cols] = acc[z, :, cols].astype(BF16)

    for w in (0, 1):
        for n in range(1, LINE):
            @pl.when(LINE - 1 - height(w) == n)
            def _():
                sent(out_stage.at[w, 0:n], usend.at[w])
    sent(back.at[0:1, :, 0 : sizes[0], :], bsend.at[0])
    sent(back.at[1:LINE], bsend.at[1])


def left_over(strips):
    return strips // 4


def flush_kernel(
    mixed, gg, gu, gd, tok, cot, hid, ggrad, ugrad, mixed_out, gg_out, gu_out, gd_out, last, sem
):
    units, width = gg.shape[1:]
    late = last.shape[1] * last.shape[3]
    strip = last.shape[3]
    early = width - late
    rows = units // PARTS
    copies = [pltpu.make_async_copy(mixed, mixed_out, sem.at[0, 0])]
    grads = ((gg, gg_out, ggrad, tok), (gu, gu_out, ugrad, tok), (gd, gd_out, hid, cot))
    for i, (src, dst, _, _) in enumerate(grads):
        for p in range(PARTS):
            at = (0, pl.ds(p * rows, rows), pl.ds(0, early))
            copies.append(pltpu.make_async_copy(src.at[at], dst.at[at], sem.at[i + 1, p]))
    for cp in copies:
        cp.start()
    for n in range(last.shape[1]):
        cols = pl.ds(early + n * strip, strip)
        for i, (_, dst, left, right) in enumerate(grads):
            r = right[:, :, :, cols].reshape(left.shape[1], strip)
            last[i, n] = jnp.dot(left[...], r, preferred_element_type=F32).astype(BF16)
            cp = pltpu.make_async_copy(last.at[i, n], dst.at[0, :, cols], sem.at[i + 1, PARTS + n])
            cp.start()
            copies.append(cp)
    for cp in copies:
        cp.wait()


def flush(*outs):
    units, width = outs[1].shape[1:]
    strip = 256 if width % 256 == 0 else width
    late = left_over(width // strip)
    return pl.pallas_call(
        flush_kernel,
        name="flush",
        out_shape=tuple(jax.ShapeDtypeStruct(o.shape, o.dtype) for o in outs[:4]),
        in_specs=vmem(len(outs)),
        out_specs=tuple(hbm(4)),
        scratch_shapes=[pltpu.VMEM((3, late, units, strip), BF16), DMA((4, PARTS + late))],
        compiler_params=pltpu.CompilerParams(vmem_limit_bytes=12 << 20),
    )(*[pltpu.with_memory_space_constraint(o, pltpu.VMEM) for o in outs])


def vmem(count):
    return [pl.BlockSpec(memory_space=pltpu.VMEM)] * count


def hbm(count):
    return [pl.BlockSpec(memory_space=pl.ANY)] * count


DMA = pltpu.SemaphoreType.DMA


def planar(pool, select, reward_w, routes, gates, target, w_gate, w_up, w_down):
    experts = LINE * PLANE
    sel_rows, top = routes.shape
    capacity = 5 * sel_rows * top // (4 * experts)
    pad = max(chunks(capacity)[1])
    half = target.shape[1]
    units, width = w_gate.shape[1:]
    span = PLANE * pad
    grad_shape = pltpu.VMEM(w_gate.shape, BF16)
    rw = reward_w.reshape(half // 128, 128)
    slots = pltpu.VMEM((LINE, PLANE, pad, width), BF16)
    act = pltpu.VMEM((LINE, units, span), F32)
    flat = pltpu.VMEM((units, experts * pad), BF16)
    outs = pl.pallas_call(
        functools.partial(layer_kernel, capacity, pad),
        name="layer",
        out_shape=(
            pltpu.VMEM((sel_rows, half), BF16), grad_shape, grad_shape, grad_shape,
            slots, slots, flat, flat, flat,
        ),
        in_specs=hbm(9),
        out_specs=tuple(vmem(9)),
        scratch_shapes=[
            pltpu.VMEM(pool.shape, BF16), pltpu.VMEM((1, sel_rows), jnp.int32),
            pltpu.VMEM(rw.shape, BF16), pltpu.VMEM((top, sel_rows), jnp.int32),
            pltpu.VMEM((top, sel_rows), F32), act, act, slots,
            pltpu.VMEM((2, LINE, sel_rows, half), BF16),
            pltpu.VMEM((LINE, 2 * experts, sel_rows), F32),
            pltpu.VMEM((LINE, experts, sel_rows), F32),
            pltpu.VMEM((16, sel_rows), F32),
            pltpu.VMEM((16, sel_rows), F32),
            pltpu.VMEM((2, LINE, 3, pad, half), BF16),
            pltpu.VMEM((LINE, PLANE, pad, half), BF16),
            pltpu.VMEM((LINE, 3, pad, half), BF16),
            pltpu.VMEM((LINE, PLANE, pad, half), BF16),
            pltpu.VMEM((LINE, sel_rows, half), F32),
            pltpu.VMEM((2, LINE - 1, sel_rows, half), BF16),
            pltpu.VMEM((2, LINE - 1, sel_rows, half), BF16),
            DMA((9,)),
            DMA((2,)), DMA((2, LINE)), DMA((2,)), DMA((LINE,)),
            DMA((2,)), DMA((LINE,)), DMA((2,)), DMA((2, LINE)),
            DMA((2, 2)), DMA((2, LINE)), DMA, DMA,
            DMA((2,)), DMA((LINE,)), DMA((2,)), DMA((LINE, PARTS)),
            DMA((2,)), DMA((2, LINE - 1, PARTS)),
        ],
        compiler_params=pltpu.CompilerParams(
            collective_id=0, has_side_effects=True, vmem_limit_bytes=44 * 10**6
        ),
    )(pool, select.reshape(1, sel_rows), rw, routes.T, gates.T, target,
      w_gate, w_up, w_down)
    return flush(*outs)


def solution(mesh):
    in_specs = (
        P("dp", "tensor"), P("dp"), P("tensor"), P("dp", None), P("dp", None), P("dp", "tensor"),
        P("dp", "tensor", None), P("dp", "tensor", None), P("dp", "tensor", None),
    )
    out_specs = (
        P("dp", "tensor"), P("dp", "tensor", None), P("dp", "tensor", None),
        P("dp", "tensor", None),
    )
    dp, tensor = mesh.shape["dp"], mesh.shape["tensor"]
    fits = tensor == 2 and dp == LINE * PLANE
    local = planar if fits else generic
    return jax.shard_map(local, mesh=mesh, in_specs=in_specs, out_specs=out_specs, check_vma=False)
```

```python
import functools
import jax
import jax.numpy as jnp
from jax import lax
from jax.experimental import pallas as pl
from jax.experimental.pallas import tpu as pltpu
from jax.sharding import PartitionSpec as P

MESH = pl.DeviceIdType.MESH
PLANE = 4
LINE = 4
PARTS = 2
CUTS = 1
F32 = jnp.float32
BF16 = jnp.bfloat16


def slot_factor(route_hit, weights):
    return jnp.sum(jnp.where(route_hit, weights.reshape(-1)[:, None], 0.0), axis=0)


def generic(pool, select, reward_w, routes, gates, target, w_gate, w_up, w_down):
    pool_rows = pool.shape[0]
    local_rows = select - lax.axis_index("dp") * pool_rows
    chosen = jnp.take(pool, local_rows, axis=0)
    sel_rows, top_count = routes.shape
    owners = lax.axis_size("dp")
    exp_dev = w_gate.shape[0]
    experts = owners * exp_dev
    capacity = 5 * sel_rows * top_count // (4 * experts)
    slot_count = experts * capacity
    flat_routes = routes.reshape(-1)
    onehot = (flat_routes[:, None] == jnp.arange(experts, dtype=jnp.int32)[None, :]).astype(
        jnp.int32
    )
    before = jnp.cumsum(onehot, axis=0) - onehot
    slot_rank = jnp.sum(before * onehot, axis=1)
    slot_place = flat_routes * capacity + slot_rank
    route_hit = slot_place[:, None] == jnp.arange(slot_count, dtype=jnp.int32)[None, :]
    route_pick = route_hit.astype(jnp.bfloat16).reshape(sel_rows, top_count, slot_count)
    token_pick = jnp.sum(route_pick, axis=1)
    reward = lax.psum(jnp.dot(chosen, reward_w, preferred_element_type=jnp.float32), "tensor")
    keep_scale = jax.nn.sigmoid(reward)
    slot_scale = slot_factor(route_hit, keep_scale[:, None] * gates)
    token_send = jnp.einsum(
        "sp,sd->pd", token_pick, chosen, preferred_element_type=jnp.float32
    ).astype(jnp.bfloat16)
    picked_target = jnp.einsum("sp,sd->pd", token_pick, target, preferred_element_type=jnp.float32)
    cot_send = (picked_target * slot_scale[:, None]).astype(jnp.bfloat16)
    token_part, cot_part = (
        lax.all_to_all(token_send, "dp", split_axis=0, concat_axis=0, tiled=True),
        lax.all_to_all(cot_send, "dp", split_axis=0, concat_axis=0, tiled=True),
    )
    received_tokens, received_cots = (
        lax.all_gather(token_part, "tensor", axis=1, tiled=True),
        lax.all_gather(cot_part, "tensor", axis=1, tiled=True),
    )
    width = received_tokens.shape[1]
    token_rows = received_tokens.reshape(owners, exp_dev, capacity, width)
    cot_rows = received_cots.reshape(owners, exp_dev, capacity, width)
    gate_act = jnp.einsum("secd,efd->secf", token_rows, w_gate, preferred_element_type=jnp.float32)
    up_act = jnp.einsum("secd,efd->secf", token_rows, w_up, preferred_element_type=jnp.float32)
    sigmoid_gate = jax.nn.sigmoid(gate_act)
    hidden = (gate_act * sigmoid_gate * up_act).astype(jnp.bfloat16)
    partial_value = jnp.einsum("secf,efd->secd", hidden, w_down, preferred_element_type=jnp.float32)
    summed = lax.psum_scatter(
        partial_value.astype(jnp.bfloat16), "tensor", scatter_dimension=3, tiled=True
    )
    returned = lax.all_to_all(summed, "dp", split_axis=0, concat_axis=0, tiled=True).reshape(
        slot_count, -1
    )
    route_rows = jnp.einsum("skp,pd->skd", route_pick, returned, preferred_element_type=jnp.float32)
    mixed = jnp.sum(route_rows * gates[:, :, None], axis=1).astype(jnp.bfloat16)
    hidden_grad = jnp.einsum("secd,efd->secf", cot_rows, w_down, preferred_element_type=jnp.float32)
    gate_grad = (
        hidden_grad * up_act * sigmoid_gate * (1.0 + gate_act * (1.0 - sigmoid_gate))
    ).astype(jnp.bfloat16)
    up_grad = (hidden_grad * gate_act * sigmoid_gate).astype(jnp.bfloat16)
    grad_down = jnp.einsum(
        "secf,secd->efd", hidden, cot_rows, preferred_element_type=jnp.float32
    ).astype(jnp.bfloat16)
    grad_gate = jnp.einsum(
        "secf,secd->efd", gate_grad, token_rows, preferred_element_type=jnp.float32
    ).astype(jnp.bfloat16)
    grad_up = jnp.einsum(
        "secf,secd->efd", up_grad, token_rows, preferred_element_type=jnp.float32
    ).astype(jnp.bfloat16)
    return (mixed, grad_gate, grad_up, grad_down)


def place():
    d = lax.axis_index("dp")
    c = lax.axis_index("tensor")
    z, q = d // PLANE, d % PLANE
    y, x = q // 2, q % 2
    mates = [((y + ry) % 2) * 2 + (x + rx) % 2 for ry, rx in ((0, 1), (1, 0), (1, 1))]
    return d, c, z, q, mates


def greet(d, c, z, q, mates):
    barrier = pltpu.get_barrier_semaphore()
    for m in mates:
        pl.semaphore_signal(barrier, inc=1, device_id=(z * PLANE + m, c), device_id_type=MESH)
    pl.semaphore_signal(barrier, inc=1, device_id=(d, 1 - c), device_id_type=MESH)

    @pl.when(z > 0)
    def _():
        pl.semaphore_signal(barrier, inc=1, device_id=(d - PLANE, c), device_id_type=MESH)

    @pl.when(z < LINE - 1)
    def _():
        pl.semaphore_signal(barrier, inc=1, device_id=(d + PLANE, c), device_id_type=MESH)


def greeted(z):
    below, above = (z + LINE - 1) // LINE, (2 * LINE - 2 - z) // LINE
    pl.semaphore_wait(pltpu.get_barrier_semaphore(), 4 + below + above)


def remote(src, dst, send, recv, dev):
    return pltpu.make_async_remote_copy(
        src_ref=src, dst_ref=dst, send_sem=send, recv_sem=recv, device_id=dev, device_id_type=MESH
    )


def sigmoid(v):
    return 1.0 / (1.0 + jnp.exp(-v))


def chunks(capacity):
    ends = [(j + 1) * capacity // 16 * 16 for j in range(LINE - 1)]
    ends.append(-(-LINE * capacity // 16) * 16)
    offs = [0] + ends[:-1]
    return offs, [b - a for a, b in zip(offs, ends)]


def layer_kernel(
    capacity, pad, pool_hbm, sel_hbm, rw_hbm, rt_hbm, gt_hbm, target_hbm, wg_hbm, wu_hbm, wd_hbm,
    mixed_ref, gg_ref, gu_ref, gd_ref, tok, cot, hid, ggrad, ugrad,
    pool_ref, sel_ref, rw_ref, rt_ref, gt_ref, gate_act, up_act, val,
    data, side_ref, scale, part, part_in, stage,
    partner_in, back, plane_in, acc, out_stage, line_in,
    lsem, zsend, zrecv, ssend, srecv, csend, crecv, xsend, xrecv, tsend, trecv, psend, precv,
    vsend, vrecv, bsend, brecv, usend, urecv, gsend, grecv,
):
    d, c, z, q, mates = place()
    experts = LINE * PLANE
    sel_rows, half = mixed_ref.shape
    top = gt_hbm.shape[0]
    wg, wu, wd = gg_ref.at[0], gu_ref.at[0], gd_ref.at[0]
    units, width = wg.shape
    span = PLANE * pad
    offs, sizes = chunks(capacity)
    rows = (tok, cot)
    mine = pl.ds(pl.multiple_of(c * half, half), half)
    other = pl.ds(pl.multiple_of((1 - c) * half, half), half)
    partner = (d, 1 - c)
    seq = (z, z + 1 - 2 * (z % 2), 2 - z // 2, 3 - 3 * (z // 2))
    piece = half // PARTS
    nt = (((1,), (1,)), ((), ()))
    tn = (((0,), (0,)), ((), ()))

    greet(d, c, z, q, mates)
    loads = [
        pltpu.make_async_copy(src, dst, lsem.at[i])
        for i, (src, dst) in enumerate((
            (sel_hbm, sel_ref), (pool_hbm, pool_ref), (rt_hbm, rt_ref), (gt_hbm, gt_ref),
            (rw_hbm, rw_ref), (target_hbm, data.at[1, z]), (wg_hbm.at[0], wg), (wu_hbm.at[0], wu),
            (wd_hbm.at[0], wd),
        ))
    ]
    for i in (1, 0, 2, 3, 4):
        loads[i].start()

    def sides():
        expert_id = lax.broadcasted_iota(jnp.int32, (experts, sel_rows), 0)
        member = jnp.zeros((experts, sel_rows), F32)
        gate = jnp.zeros((experts, sel_rows), F32)
        for k in range(top):
            eq = rt_ref[k : k + 1, :] == expert_id
            member = member + jnp.where(eq, 1.0, 0.0)
            gate = gate + jnp.where(eq, gt_ref[k : k + 1, :], 0.0)
        tri = jnp.where(
            lax.broadcasted_iota(jnp.int32, (sel_rows, sel_rows), 0)
            < lax.broadcasted_iota(jnp.int32, (sel_rows, sel_rows), 1),
            1.0,
            0.0,
        ).astype(BF16)
        before = jnp.dot(member.astype(BF16), tri, preferred_element_type=F32)
        side_ref[z, 0:experts, :] = jnp.where(member > 0.5, before, -1024.0)
        side_ref[z, experts : 2 * experts, :] = gate

    loads[0].wait()
    pool_rows = pool_ref.shape[0]
    hit = (
        lax.broadcasted_iota(jnp.int32, (pool_rows, sel_rows), 0) == sel_ref[...] - d * pool_rows
    ).astype(F32).astype(BF16)
    loads[1].wait()
    loads[5].start()
    chosen = lax.dot_general(
        hit, pool_ref[...], tn, preferred_element_type=F32
    ).astype(BF16)
    data[0, z] = chosen

    def zcopy(a, s, way, kind):
        blk = z - way * s
        dev = (d + way * PLANE, c)
        w = (way + 1) // 2
        if kind == 1:
            spot = data.at[a, blk]
            return remote(spot, spot, zsend.at[w], zrecv.at[a, blk], dev)
        if a == 0:
            spot = side_ref.at[blk, 0:experts]
            return remote(spot, spot, ssend.at[w], srecv.at[blk], dev)
        if kind == 2:
            spot = side_ref.at[blk, experts : 2 * experts]
            return remote(spot, spot, gsend.at[w], grecv.at[blk], dev)
        spot = scale.at[blk]
        return remote(spot, spot, csend.at[w], crecv.at[blk], dev)

    def inside(to):
        return (z > 0) & (z < LINE - 1) & (to > 0) & (to < LINE - 1)

    def among(links, to):
        return {"all": True, "inner": inside(to), "outer": jnp.logical_not(inside(to))}[links]

    def sends(s, way):
        blk, to = z - way * s, z + way
        return (blk >= 0) & (blk < LINE) & (to >= 0) & (to < LINE)

    def zstart(a, s, which=(0, 1), links="all"):
        for way in (1, -1):
            @pl.when(sends(s, way) & among(links, z + way))
            def _():
                for i in which:
                    zcopy(a, s, way, i).start()

    def arrives(s, way):
        blk = z - way * (s + 1)
        return (blk >= 0) & (blk < LINE)

    def zwait(a, s, links="all"):
        for way in (1, -1):
            @pl.when(arrives(s, way) & among(links, z - way))
            def _():
                blk = z - way * (s + 1)
                remote(
                    data.at[a, blk], data.at[a, blk], zsend.at[0], zrecv.at[a, blk], partner
                ).wait_recv()
                if a == 0:
                    spot = side_ref.at[blk, 0:experts]
                    remote(spot, spot, ssend.at[0], srecv.at[blk], partner).wait_recv()
                else:
                    remote(
                        scale.at[blk], scale.at[blk], csend.at[0], crecv.at[blk], partner
                    ).wait_recv()

    def gates_wait(s):
        for way in (1, -1):
            @pl.when(arrives(s, way))
            def _():
                blk = z - way * (s + 1)
                spot = side_ref.at[blk, experts : 2 * experts]
                remote(spot, spot, gsend.at[0], grecv.at[blk], partner).wait_recv()

    def tcopy(a, j, m):
        spot = rows[a].at[j, m, 0 : sizes[j], mine]
        return remote(spot, spot, tsend.at[a, min(j, 1)], trecv.at[a, j], partner)

    def tall(a, j, side):
        spot = rows[a].at[j, :, 0 : sizes[j], side]
        return remote(spot, spot, tsend.at[a, min(j, 1)], trecv.at[a, j], partner)

    def tarrive(a, j):
        tall(a, j, other).wait_recv()

    def xcopy(a, j, r):
        return remote(
            stage.at[a, j, r, 0 : sizes[j], :],
            rows[a].at[j, q, 0 : sizes[j], mine],
            xsend.at[min(j, 1)],
            xrecv.at[a, j],
            (z * PLANE + mates[r], c),
        )

    slot_id = lax.broadcasted_iota(jnp.int32, (pad, sel_rows), 0).astype(F32)

    def pick(a, j):
        size = sizes[j]
        sources = [(seq[i], float(offs[j] - capacity * i)) for i in ((j, j - 1) if j else (j,))]
        sides = (2, 0, 1, 3)
        hits, factors = [], []
        for r in sides:
            e = z * PLANE + (mates[r] if r < 3 else q)
            ms = [slot_id[:size] + base == side_ref[b, pl.ds(e, 1), :] for b, base in sources]
            hits.append(jnp.concatenate([jnp.where(m, 1.0, 0.0) for m in ms], axis=1))
            if a == 1:
                total = sum(
                    jnp.where(m, scale[b, pl.ds(e, 1), :], 0.0) for m, (b, _) in zip(ms, sources)
                )
                factors.append(jnp.sum(total, axis=1, keepdims=True))
        hits = jnp.concatenate(hits, axis=0).astype(BF16)
        if a == 1:
            factors = jnp.concatenate(factors, axis=0)
        cut = 256 if half % 256 == 0 else half
        for n in range(half // cut):
            cols = pl.ds(n * cut, cut)
            source = jnp.concatenate([data[a, b, :, cols] for b, _ in sources], axis=0)
            picked = jnp.dot(hits, source, preferred_element_type=F32)
            if a == 1:
                picked = picked * factors
            picked = picked.astype(BF16)
            for i, r in enumerate(sides):
                got = picked[i * size : (i + 1) * size]
                if r < 3:
                    stage[a, j, r, 0:size, cols] = got
                else:
                    spot = pl.ds(pl.multiple_of(c * half + n * cut, cut), cut)
                    rows[a][j, q, 0:size, spot] = got
        for r in (2, 0, 1):
            xcopy(a, j, r).start()
        tcopy(a, j, q).start()

    def forward(a, j):
        remote(
            stage.at[a, j, :, 0 : sizes[j], :], rows[a].at[j, 0:3, 0 : sizes[j], mine],
            xsend.at[min(j, 1)], xrecv.at[a, j], partner,
        ).wait_recv()
        for m in mates:
            tcopy(a, j, m).start()

    def vcopy(j):
        return remote(
            val.at[j, :, 0 : sizes[j], other], partner_in.at[j, :, 0 : sizes[j], :],
            vsend.at[min(j, 1)], vrecv.at[j], partner,
        )

    tile = 512 if half % 512 == 0 else half

    def group(j):
        lanes = pl.ds(j * span, span)
        tarrive(0, j)
        x = tok[j].reshape(span, width)
        g = lax.dot_general(wg[...], x, nt, preferred_element_type=F32)
        u = lax.dot_general(wu[...], x, nt, preferred_element_type=F32)
        gate_act[j] = g
        up_act[j] = u
        h = (g * sigmoid(g) * u).astype(BF16)
        hid[:, lanes] = h
        for side in (1 - c, c):
            for n in range(half // tile):
                cols = pl.ds(pl.multiple_of(side * half + n * tile, tile), tile)
                v = lax.dot_general(h, wd[:, cols], tn, preferred_element_type=F32)
                val[j, :, :, cols] = v.astype(BF16).reshape(PLANE, pad, tile)
            if side is not c:
                vcopy(j).start()

    def grad_group(j):
        lanes = pl.ds(j * span, span)
        tarrive(1, j)
        x = cot[j].reshape(span, width)
        hg = lax.dot_general(wd[...], x, nt, preferred_element_type=F32)
        g = gate_act[j]
        s = sigmoid(g)
        ggrad[:, lanes] = (hg * up_act[j] * s * (1.0 + g * (1.0 - s))).astype(BF16)
        ugrad[:, lanes] = (hg * g * s).astype(BF16)

    grads = ((ggrad, tok, wg), (ugrad, tok, wu), (hid, cot, wd))
    strip = 256 if width % 256 == 0 else width
    strips = width // strip - left_over(width // strip)

    def grad_strip(n, carry):
        cols = pl.ds(pl.multiple_of(n * strip, strip), strip)
        for left, right, out in grads:
            r = right[:, :, :, cols].reshape(experts * pad, strip)
            out[:, cols] = jnp.dot(left[...], r, preferred_element_type=F32).astype(BF16)
        return carry

    def bcopy(j, r, h):
        cols = pl.ds(h * piece, piece)
        return remote(
            back.at[j, r, 0 : sizes[j], cols], plane_in.at[j, q, 0 : sizes[j], cols],
            bsend.at[min(j, 1)], brecv.at[j, h],
            (z * PLANE + mates[r], c),
        )

    def give(j):
        size = sizes[j]
        vcopy(j).wait_recv()
        for h in range(PARTS):
            cols = pl.ds(h * piece, piece)
            spot = pl.ds(pl.multiple_of(c * half + h * piece, piece), piece)
            for r in (2, 0, 1, 3):
                m = mates[r] if r < 3 else q
                total = (
                    val[j, m, 0:size, spot].astype(F32) + partner_in[j, m, 0:size, cols].astype(F32)
                ).astype(BF16)
                if r < 3:
                    back[j, r, 0:size, cols] = total
                    bcopy(j, r, h).start()
                else:
                    plane_in[j, q, 0:size, cols] = total

    def mixing(j):
        blk = seq[j]
        weights, takes = [], []
        for m in range(PLANE):
            e = z * PLANE + m
            rank = side_ref[blk, pl.ds(e, 1), :]
            strength = side_ref[blk, pl.ds(experts + e, 1), :]
            spots = [(j, sizes[j])] + ([(j + 1, 16)] if j + 1 < LINE else [])
            for i, size in spots:
                base = float(offs[i] - capacity * j)
                w = jnp.where(slot_id[:size] + base == rank, strength, 0.0)
                high = w.astype(BF16)
                weights += [high, (w - high.astype(F32)).astype(BF16)]
                takes += [(i, m, size)] * 2
        return jnp.concatenate(weights, axis=0), takes

    def combine(j, h, mix):
        weights, takes = mix
        cols = pl.ds(h * piece, piece)
        remote(
            back.at[j, :, 0 : sizes[j], cols], plane_in.at[j, 0:3, 0 : sizes[j], cols],
            bsend.at[min(j, 1)], brecv.at[j, h], partner,
        ).wait_recv()
        values = jnp.concatenate([plane_in[i, m, 0:size, cols] for i, m, size in takes], axis=0)
        acc[seq[j], :, cols] = lax.dot_general(weights, values, tn, preferred_element_type=F32)

    def ucopy(w, s, h):
        cols = pl.ds(h * piece, piece)
        to = d + (2 * w - 1) * PLANE
        return remote(
            out_stage.at[w, s, :, cols], line_in.at[w, s, :, cols], usend.at[w],
            urecv.at[w, s, h], (to, c),
        )

    def height(w):
        return z if w == 1 else LINE - 1 - z

    def lifts(w, s):
        return (height(w) <= s) & (height(w) < LINE - 1)

    def lands(w, s):
        return (height(w) > 0) & (height(w) - 1 <= s)

    def lift(s, h):
        cols = pl.ds(h * piece, piece)
        for w in (1, 0):
            blk = z + (2 * w - 1) * (LINE - 1 - s)
            if s > 0:
                @pl.when(lands(w, s - 1))
                def _():
                    ucopy(w, s - 1, h).wait_recv()

                @pl.when(lifts(w, s) & (height(w) > 0))
                def _():
                    out_stage[w, s, :, cols] = (
                        acc[blk, :, cols] + line_in[w, s - 1, :, cols].astype(F32)
                    ).astype(BF16)
                    ucopy(w, s, h).start()

            @pl.when(lifts(w, s) & (height(w) == 0))
            def _():
                out_stage[w, s, :, cols] = acc[blk, :, cols].astype(BF16)
                ucopy(w, s, h).start()

    def rewards():
        rw = rw_ref[...].astype(F32)
        rw_rows = jnp.concatenate(
            [jnp.broadcast_to(rw[i : i + 1, :], (16, rw.shape[1])) for i in range(rw.shape[0])],
            axis=1,
        ).astype(BF16)
        part[...] = lax.dot_general(rw_rows, data[0, z], nt, preferred_element_type=F32)

    reward_copy = remote(part, part_in, psend, precv, partner)
    greeted(z)
    zstart(0, 0, (1,))
    loads[2].wait()
    loads[3].wait()
    sides()
    zstart(0, 0, (0,))
    pick(0, 0)
    loads[5].wait()
    zstart(1, 0, (1,), "outer")
    for cp in loads[6:9]:
        cp.start()
    loads[4].wait()
    rewards()
    reward_copy.start()
    for j in range(LINE):
        if sizes[j] < pad:
            for a in (0, 1):
                rows[a][j, :, sizes[j] : pad, :] = jnp.zeros(
                    (PLANE, pad - sizes[j], width), BF16
                )
    reward_copy.wait()
    scale[z] = sigmoid(part[0:1, :] + part_in[0:1, :]) * side_ref[z, experts : 2 * experts, :]
    zstart(1, 0, (0,))
    pick(1, 0)
    forward(0, 0)
    zwait(0, 0)
    zstart(0, 1)
    zstart(1, 0, (1,), "inner")
    pick(0, 1)
    for cp in loads[6:9]:
        cp.wait()
    group(0)
    forward(1, 0)
    zwait(1, 0, "outer")
    pick(1, 1)
    grad_group(0)
    forward(0, 1)
    zwait(0, 1)
    zstart(0, 2)
    zstart(1, 1, links="inner")
    pick(0, 2)
    group(1)
    forward(1, 1)
    zwait(1, 0, "inner")
    zstart(1, 1, links="outer")
    zwait(0, 2)
    pick(0, 3)
    grad_group(1)
    forward(0, 2)
    zwait(1, 1)
    zstart(1, 2)
    zstart(1, 0, (2,))
    pick(1, 2)
    group(2)
    forward(0, 3)
    zwait(1, 2)
    pick(1, 3)
    gates_wait(0)
    zstart(1, 1, (2,))
    group(3)
    for j in (3, 2, 1, 0):
        give(j)
    forward(1, 2)
    gates_wait(1)
    zstart(1, 2, (2,))
    grad_group(2)
    forward(1, 3)
    grad_group(3)
    gates_wait(2)

    last = LINE - 2
    done, turn = 0, 0
    for s in range(LINE - 1):
        j = LINE - 1 - s
        mix = mixing(j)
        for h in range(PARTS):
            combine(j, h, mix)
            lift(s, h)
            upto = min(2 * turn + 1, strips)
            if upto > done:
                lax.fori_loop(done, upto, grad_strip, 0)
                done = upto
            turn = turn + 1
    lax.fori_loop(done, strips, grad_strip, 0)

    def sent(src, sem):
        remote(src, src, sem, vrecv.at[0], partner).wait_send()

    for w in (0, 1):
        for n in range(1, LINE):
            @pl.when(LINE - height(1 - w) == n)
            def _():
                sent(data.at[:, 0:n], zsend.at[w])
                sent(side_ref.at[0:n, 0:experts], ssend.at[w])
                sent(side_ref.at[0:n, experts : 2 * experts], gsend.at[w])
                sent(scale.at[0:n], csend.at[w])
    for i, cut in ((0, slice(0, 1)), (1, slice(1, LINE))):
        size = sizes[0] if i == 0 else pad
        sent(stage.at[:, cut, :, 0:size, :], xsend.at[i])
        sent(val.at[cut, :, 0:size, other], vsend.at[i])
        for a in (0, 1):
            sent(rows[a].at[cut, :, 0:size, mine], tsend.at[a, i])

    mix = mixing(0)
    for h in range(PARTS):
        combine(0, h, mix)
        cols = pl.ds(h * piece, piece)
        for w in (1, 0):
            @pl.when(lands(w, last))
            def _():
                ucopy(w, last, h).wait_recv()
                acc[z, :, cols] = acc[z, :, cols] + line_in[w, last, :, cols].astype(F32)
        mixed_ref[:, cols] = acc[z, :, cols].astype(BF16)

    for w in (0, 1):
        for n in range(1, LINE):
            @pl.when(LINE - 1 - height(w) == n)
            def _():
                sent(out_stage.at[w, 0:n], usend.at[w])
    sent(back.at[0:1, :, 0 : sizes[0], :], bsend.at[0])
    sent(back.at[1:LINE], bsend.at[1])


def left_over(strips):
    return strips // 4


def flush_kernel(
    mixed, gg, gu, gd, tok, cot, hid, ggrad, ugrad, mixed_out, gg_out, gu_out, gd_out, last, sem
):
    units, width = gg.shape[1:]
    late = last.shape[1] * last.shape[3]
    strip = last.shape[3]
    early = width - late
    rows = units // CUTS
    copies = [pltpu.make_async_copy(mixed, mixed_out, sem.at[0, 0])]
    grads = ((gg, gg_out, ggrad, tok), (gu, gu_out, ugrad, tok), (gd, gd_out, hid, cot))
    for i, (src, dst, _, _) in enumerate(grads):
        for p in range(CUTS):
            at = (0, pl.ds(p * rows, rows), pl.ds(0, early))
            copies.append(pltpu.make_async_copy(src.at[at], dst.at[at], sem.at[i + 1, p]))
    for cp in copies:
        cp.start()
    for n in range(last.shape[1]):
        cols = pl.ds(early + n * strip, strip)
        for i, (_, dst, left, right) in enumerate(grads):
            r = right[:, :, :, cols].reshape(left.shape[1], strip)
            last[i, n] = jnp.dot(left[...], r, preferred_element_type=F32).astype(BF16)
            cp = pltpu.make_async_copy(last.at[i, n], dst.at[0, :, cols], sem.at[i + 1, CUTS + n])
            cp.start()
            copies.append(cp)
    for cp in copies:
        cp.wait()


def flush(*outs):
    units, width = outs[1].shape[1:]
    strip = 256 if width % 256 == 0 else width
    late = left_over(width // strip)
    return pl.pallas_call(
        flush_kernel,
        name="flush",
        out_shape=tuple(jax.ShapeDtypeStruct(o.shape, o.dtype) for o in outs[:4]),
        in_specs=vmem(len(outs)),
        out_specs=tuple(hbm(4)),
        scratch_shapes=[pltpu.VMEM((3, late, units, strip), BF16), DMA((4, CUTS + late))],
        compiler_params=pltpu.CompilerParams(vmem_limit_bytes=12 << 20),
    )(*[pltpu.with_memory_space_constraint(o, pltpu.VMEM) for o in outs])


def vmem(count):
    return [pl.BlockSpec(memory_space=pltpu.VMEM)] * count


def hbm(count):
    return [pl.BlockSpec(memory_space=pl.ANY)] * count


DMA = pltpu.SemaphoreType.DMA


def planar(pool, select, reward_w, routes, gates, target, w_gate, w_up, w_down):
    experts = LINE * PLANE
    sel_rows, top = routes.shape
    capacity = 5 * sel_rows * top // (4 * experts)
    pad = max(chunks(capacity)[1])
    half = target.shape[1]
    units, width = w_gate.shape[1:]
    span = PLANE * pad
    grad_shape = pltpu.VMEM(w_gate.shape, BF16)
    rw = reward_w.reshape(half // 128, 128)
    slots = pltpu.VMEM((LINE, PLANE, pad, width), BF16)
    act = pltpu.VMEM((LINE, units, span), F32)
    flat = pltpu.VMEM((units, experts * pad), BF16)
    outs = pl.pallas_call(
        functools.partial(layer_kernel, capacity, pad),
        name="layer",
        out_shape=(
            pltpu.VMEM((sel_rows, half), BF16), grad_shape, grad_shape, grad_shape,
            slots, slots, flat, flat, flat,
        ),
        in_specs=hbm(9),
        out_specs=tuple(vmem(9)),
        scratch_shapes=[
            pltpu.VMEM(pool.shape, BF16), pltpu.VMEM((1, sel_rows), jnp.int32),
            pltpu.VMEM(rw.shape, BF16), pltpu.VMEM((top, sel_rows), jnp.int32),
            pltpu.VMEM((top, sel_rows), F32), act, act, slots,
            pltpu.VMEM((2, LINE, sel_rows, half), BF16),
            pltpu.VMEM((LINE, 2 * experts, sel_rows), F32),
            pltpu.VMEM((LINE, experts, sel_rows), F32),
            pltpu.VMEM((16, sel_rows), F32),
            pltpu.VMEM((16, sel_rows), F32),
            pltpu.VMEM((2, LINE, 3, pad, half), BF16),
            pltpu.VMEM((LINE, PLANE, pad, half), BF16),
            pltpu.VMEM((LINE, 3, pad, half), BF16),
            pltpu.VMEM((LINE, PLANE, pad, half), BF16),
            pltpu.VMEM((LINE, sel_rows, half), F32),
            pltpu.VMEM((2, LINE - 1, sel_rows, half), BF16),
            pltpu.VMEM((2, LINE - 1, sel_rows, half), BF16),
            DMA((9,)),
            DMA((2,)), DMA((2, LINE)), DMA((2,)), DMA((LINE,)),
            DMA((2,)), DMA((LINE,)), DMA((2,)), DMA((2, LINE)),
            DMA((2, 2)), DMA((2, LINE)), DMA, DMA,
            DMA((2,)), DMA((LINE,)), DMA((2,)), DMA((LINE, PARTS)),
            DMA((2,)), DMA((2, LINE - 1, PARTS)), DMA((2,)), DMA((LINE,)),
        ],
        compiler_params=pltpu.CompilerParams(
            collective_id=0, has_side_effects=True, vmem_limit_bytes=44 * 10**6
        ),
    )(pool, select.reshape(1, sel_rows), rw, routes.T, gates.T, target,
      w_gate, w_up, w_down)
    return flush(*outs)


def solution(mesh):
    in_specs = (
        P("dp", "tensor"), P("dp"), P("tensor"), P("dp", None), P("dp", None), P("dp", "tensor"),
        P("dp", "tensor", None), P("dp", "tensor", None), P("dp", "tensor", None),
    )
    out_specs = (
        P("dp", "tensor"), P("dp", "tensor", None), P("dp", "tensor", None),
        P("dp", "tensor", None),
    )
    dp, tensor = mesh.shape["dp"], mesh.shape["tensor"]
    fits = tensor == 2 and dp == LINE * PLANE
    local = planar if fits else generic
    return jax.shard_map(local, mesh=mesh, in_specs=in_specs, out_specs=out_specs, check_vma=False)
```
